32 devices in a mesh: dp: 16 (over z, x, core), ctx: 2 (over y).
Axes of the slice: x: 2, y: 2, z: 4, core: 2. Of those that a mesh axis runs over, the one named last changes fastest.
Arguments:
- block_input: bfloat16 [16, 256, 768], P('dp', 'ctx'), may hold values from -6 to 6
- out_grad: bfloat16 [16, 256, 768], P('dp', 'ctx'), may hold values from -6 to 6
- positions: int32 [16, 256], P('dp', 'ctx'), may hold values from 0 to 255, as said below
- w_qkv: float32 [768, 2304], P('dp'), may hold values from -0.3125 to 0.3125
- w_attn_out: float32 [768, 768], P('dp'), may hold values from -0.625 to 0.625
- w_in: float32 [768, 2304], P('dp'), may hold values from -0.21875 to 0.21875
- w_mlp_out: float32 [768, 1152], P('dp'), may hold values from -0.1875 to 0.1875
- norm_gains: float32 [2, 768], P(None, 'dp'), may hold values from 0.5 to 1.5
- m_qkv: float32 [768, 2304], P('dp'), may hold values from -0.9 to 0.9
- m_attn_out: float32 [768, 768], P('dp'), may hold values from -0.9 to 0.9
- m_in: float32 [768, 2304], P('dp'), may hold values from -0.9 to 0.9
- m_mlp_out: float32 [768, 1152], P('dp'), may hold values from -0.9 to 0.9
- gain_mean: float32 [2, 768], P(None, 'dp'), may hold values from -0.3 to 0.3
- gain_var: float32 [2, 768], P(None, 'dp'), may hold values from 0.05 to 0.5
Outputs:
- block_output: bfloat16 [16, 256, 768], P('dp', 'ctx')
- input_grad: float32 [16, 256, 768], P('dp', 'ctx')
- grad_qkv: float32 [768, 2304], P('dp')
- grad_attn_out: float32 [768, 768], P('dp')
- grad_in: float32 [768, 2304], P('dp')
- grad_mlp_out: float32 [768, 1152], P('dp')
- grad_gains: float32 [2, 768], P(None, 'dp')
- new_qkv: float32 [768, 2304], P('dp')
- new_attn_out: float32 [768, 768], P('dp')
- new_in: float32 [768, 2304], P('dp')
- new_mlp_out: float32 [768, 1152], P('dp')
- new_gains: float32 [2, 768], P(None, 'dp')
- new_m_qkv: float32 [768, 2304], P('dp')
- new_m_attn_out: float32 [768, 768], P('dp')
- new_m_in: float32 [768, 2304], P('dp')
- new_m_mlp_out: float32 [768, 1152], P('dp')
- new_gain_mean: float32 [2, 768], P(None, 'dp')
- new_gain_var: float32 [2, 768], P(None, 'dp')
The draws below stay inside these ranges and needn't reach their ends.
Inputs may be any that keep to these rules, and one draw needn't show every extreme that they name: In each sequence positions count up by one and restart at 0 at the first token of each packed document; every sequence begins at 0; documents vary in length and number; the first sequence is a single document.
All inputs are finite; a program needn't handle non-finite values.
Results may differ from the reference program's by a relative error of at most 0.035.
Values may be sent and summed in bfloat16 or wider, within the bound.
No kernel may reach another device: no remote copies, remote signals or barrier semaphores. Data moves between devices by JAX's collectives and lax.ppermute only.
A program may use at most 128 MiB of HBM per device.

```python
import math
import jax
import jax.numpy as jnp
from jax import lax

D = 768
HEADS = 12
FF = 1152
NS_ITERS = 5
LEN = 256
SEQS = 16
TOKENS = 4096


def draw_positions(key, part):
    cut_points = jax.random.randint(key, (SEQS, 8), 0, LEN)
    sequence_ids = jnp.arange(SEQS, dtype=jnp.int32)
    cut_points = jnp.where((sequence_ids == 0)[:, None], 0, cut_points)
    places = jnp.arange(LEN, dtype=jnp.int32)
    start_flags = jnp.any(places[None, :, None] == cut_points[:, None, :], axis=-1)
    start_flags = jnp.logical_or(start_flags, (places == 0)[None, :])
    start_marks = jnp.where(start_flags, places[None, :], 0)
    document_start = lax.cummax(start_marks, axis=1)
    return (places[None, :] - document_start).astype(jnp.int32)


def levels(key, extent, cuts, least, largest):
    def one(axis_at, blocks):
        heights = jax.random.uniform(jax.random.fold_in(jax.random.fold_in(key, 6), axis_at), (blocks,), jnp.float32, least / len(cuts), largest / len(cuts))
        return jnp.repeat(jnp.exp(heights), extent[axis_at] // blocks).reshape((-1,) + (1,) * (len(extent) - axis_at - 1))

    level = one(*cuts[0])
    for cut in cuts[1:]:
        level = level * one(*cut)
    return level


def noise(rng, extent, scale, reach, cuts=(), held_as=jnp.bfloat16):
    entries = jax.random.normal(rng, extent, jnp.float32) * scale
    if len(cuts) > 0:
        entries = levels(rng, extent, cuts, -0.22, 0.18) * entries
    return jnp.clip(entries, min=-reach, max=reach).astype(held_as)


def setup_inputs(seed: int = 0) -> dict:
    key_of = jax.random.split(jax.random.key(seed), 15)
    block_input = noise(key_of[0], (SEQS, LEN, D), 1.0, 6.0, ((0, 16), (1, 2)))
    out_grad = noise(key_of[1], (SEQS, LEN, D), 1.0, 6.0, ((0, 16), (1, 2)))
    positions = draw_positions(jax.random.fold_in(key_of[14], 71), 0)
    w_qkv = noise(key_of[3], (D, 3 * D), (D // 2) ** -0.5, 0.3125, ((0, 16),), jnp.float32)
    w_attn_out = noise(key_of[4], (D, D), (D // 8) ** -0.5, 0.625, ((0, 16),), jnp.float32)
    w_in = noise(key_of[5], (D, 2 * FF), D ** -0.5, 0.21875, ((0, 16),), jnp.float32)
    w_mlp_out = noise(key_of[6], (D, FF), FF ** -0.5, 0.1875, ((0, 16),), jnp.float32)
    norm_gains = jnp.clip(1.0 + 0.1 * jax.random.normal(key_of[7], (2, D), jnp.float32), 0.5, 1.5)
    m_qkv = noise(key_of[8], (D, 3 * D), 0.15, 0.9, ((0, 16),), jnp.float32)
    m_attn_out = noise(key_of[9], (D, D), 0.15, 0.9, ((0, 16),), jnp.float32)
    m_in = noise(key_of[10], (D, 2 * FF), 0.15, 0.9, ((0, 16),), jnp.float32)
    m_mlp_out = noise(key_of[11], (D, FF), 0.15, 0.9, ((0, 16),), jnp.float32)
    gain_mean = noise(key_of[12], (2, D), 0.05, 0.3, ((1, 16),), jnp.float32)
    gain_var = jnp.clip(jnp.exp(math.log(0.5) - 2.3025851 * jax.random.uniform(key_of[13], (2, D), jnp.float32) ** levels(key_of[13], (2, D), ((1, 16),), -0.2, 0.2)), 0.05, 0.5)
    return {"block_input": block_input, "out_grad": out_grad, "positions": positions, "w_qkv": w_qkv, "w_attn_out": w_attn_out, "w_in": w_in, "w_mlp_out": w_mlp_out, "norm_gains": norm_gains, "m_qkv": m_qkv, "m_attn_out": m_attn_out, "m_in": m_in, "m_mlp_out": m_mlp_out, "gain_mean": gain_mean, "gain_var": gain_var}


theta_base = 160000.0
norm_eps = 1e-05
quintic_one = 3.4445
quintic_two = -4.775
quintic_three = 2.0315
momentum_rate = 0.95
matrix_rate = 0.04
gain_rate = 0.1
beta_first = 0.9
beta_second = 0.95
adam_eps = 1e-08
first_fix = 1.0 - 0.9 ** 10
second_fix = 1.0 - 0.95 ** 10
ortho_eps = 1e-07

def widen(array):
    return lax.optimization_barrier(array).astype(jnp.float32)

def rope_tables(positions, head_size):
    half_size = head_size // 2
    indices = jnp.arange(half_size, dtype=jnp.float32)
    frequency = jnp.exp(indices * (-2.0 * math.log(theta_base) / head_size))
    angles = positions.astype(jnp.float32)[:, None] * frequency[None, :]
    return (jnp.cos(angles)[:, None, :], jnp.sin(angles)[:, None, :])

def rotate(field, cosine, sine):
    half_size = field.shape[-1] // 2
    first_half = field[..., :half_size]
    second_half = field[..., half_size:]
    return jnp.concatenate([first_half * cosine - second_half * sine, second_half * cosine + first_half * sine], axis=-1)

def rotate_back(gradient, cosine, sine):
    half_size = gradient.shape[-1] // 2
    first_half = gradient[..., :half_size]
    second_half = gradient[..., half_size:]
    return jnp.concatenate([first_half * cosine + second_half * sine, second_half * cosine - first_half * sine], axis=-1)

def normalize(field):
    centered = field - lax.optimization_barrier(jnp.mean(field, axis=-1, keepdims=True))
    factor = lax.rsqrt(lax.optimization_barrier(jnp.mean(centered * centered, axis=-1, keepdims=True)) + norm_eps)
    return (centered * factor, factor)

def normalize_back(grad_hat, normed, factor):
    first_mean = lax.optimization_barrier(jnp.mean(grad_hat, axis=-1, keepdims=True))
    second_mean = lax.optimization_barrier(jnp.mean(grad_hat * normed, axis=-1, keepdims=True))
    return factor * (grad_hat - first_mean - normed * second_mean)

def gelu_parts(preact):
    cumulative = 0.5 * (1.0 + lax.erf(preact * (1.0 / math.sqrt(2.0))))
    activated = preact * cumulative
    derivative = cumulative + preact * jnp.exp(-0.5 * preact * preact) * (1.0 / math.sqrt(2.0 * math.pi))
    return (activated, derivative)

def contract_rows(left_side, right_side):
    return lax.dot_general(left_side, right_side, (((0,), (0,)), ((), ())), preferred_element_type=jnp.float32)

def contract_cols(left_side, right_side):
    return lax.dot_general(left_side, right_side, (((1,), (1,)), ((), ())), preferred_element_type=jnp.float32)

def sequence_pass(params, x_seq, dy_seq, pos_seq):
    w_qkv_b, w_out_b, w_in_b, w_mlp_b, gains_b = params
    length, width = x_seq.shape
    heads = HEADS
    head_size = width // heads
    score_scale = 1.0 / math.sqrt(head_size)
    gain_one = gains_b[0].astype(jnp.float32)
    gain_two = gains_b[1].astype(jnp.float32)
    x_wide = x_seq.astype(jnp.float32)
    hat_one, factor_one = normalize(x_wide)
    act_one = (hat_one * gain_one).astype(jnp.bfloat16)
    qkv = jnp.dot(act_one, w_qkv_b, preferred_element_type=jnp.float32)
    cosine, sine = rope_tables(pos_seq, head_size)
    doc_start = jnp.arange(length, dtype=jnp.int32) - pos_seq.astype(jnp.int32)
    queries_b = rotate(qkv[:, :width].reshape(length, heads, head_size), cosine, sine).astype(jnp.bfloat16)
    keys_b = rotate(qkv[:, width:2 * width].reshape(length, heads, head_size), cosine, sine).astype(jnp.bfloat16)
    values_b = qkv[:, 2 * width:].reshape(length, heads, head_size).astype(jnp.bfloat16)
    keys_wide = widen(keys_b)
    values_wide = widen(values_b)
    block_rows = math.gcd(length, 512)
    block_count = length // block_rows

    def forward_block(pieces):
        query_block, doc_block = pieces
        same = (doc_block[:, None] == doc_start[None, :])[None]
        scores = jnp.einsum('qhd,khd->hqk', widen(query_block), keys_wide) * score_scale
        weights = jnp.where(same, jnp.exp(scores), 0.0)
        totals = lax.optimization_barrier(jnp.sum(weights, axis=-1))
        summed = jnp.einsum('hqk,khd->qhd', widen(weights.astype(jnp.bfloat16)), values_wide)
        return (summed / jnp.transpose(totals)[:, :, None], jnp.log(totals))
    doc_blocks = doc_start.reshape(block_count, block_rows)
    attended, log_total = lax.map(forward_block, (queries_b.reshape(block_count, block_rows, heads, head_size), doc_blocks))
    attended = attended.reshape(length, heads, head_size)
    mixed_b = attended.reshape(length, width).astype(jnp.bfloat16)
    hidden = x_wide + jnp.dot(mixed_b, w_out_b, preferred_element_type=jnp.float32)
    hat_two, factor_two = normalize(hidden)
    act_two = (hat_two * gain_two).astype(jnp.bfloat16)
    lifted = jnp.dot(act_two, w_in_b, preferred_element_type=jnp.float32)
    hidden_units = lifted.shape[1] // 2
    preact = lifted[:, :hidden_units]
    gate_half = lifted[:, hidden_units:]
    activated, derivative = gelu_parts(preact)
    inner_b = (activated * gate_half).astype(jnp.bfloat16)
    output = hidden + contract_cols(inner_b, w_mlp_b)
    dy_wide = dy_seq.astype(jnp.float32)
    grad_mlp = contract_rows(dy_seq, inner_b)
    grad_inner = jnp.dot(dy_seq, w_mlp_b, preferred_element_type=jnp.float32)
    grad_lift = jnp.concatenate([grad_inner * gate_half * derivative, grad_inner * activated], axis=1).astype(jnp.bfloat16)
    grad_in = contract_rows(act_two, grad_lift)
    grad_act_two = contract_cols(grad_lift, w_in_b)
    gain_grad_two = lax.optimization_barrier(jnp.sum(grad_act_two * hat_two, axis=0))
    grad_hidden = dy_wide + normalize_back(grad_act_two * gain_two, hat_two, factor_two)
    grad_hidden_b = grad_hidden.astype(jnp.bfloat16)
    grad_out = contract_rows(mixed_b, grad_hidden_b)
    grad_mixed = contract_cols(grad_hidden_b, w_out_b).reshape(length, heads, head_size)
    delta = lax.optimization_barrier(jnp.sum(grad_mixed * attended, axis=-1))
    grad_mixed_b = grad_mixed.astype(jnp.bfloat16)

    def backward_block(carry, pieces):
        key_acc, value_acc = carry
        query_block, grad_block, delta_block, log_block, doc_block = pieces
        same = (doc_block[:, None] == doc_start[None, :])[None]
        query_wide = widen(query_block)
        grad_wide = widen(grad_block)
        scores = jnp.einsum('qhd,khd->hqk', query_wide, keys_wide) * score_scale
        probs = jnp.where(same, jnp.exp(scores - log_block[:, :, None]), 0.0)
        value_acc = value_acc + jnp.einsum('hqk,qhd->khd', widen(probs.astype(jnp.bfloat16)), grad_wide)
        grad_probs = jnp.einsum('qhd,khd->hqk', grad_wide, values_wide)
        grad_scores = probs * (grad_probs - jnp.transpose(delta_block)[:, :, None])
        grad_scores_w = widen(grad_scores.astype(jnp.bfloat16))
        query_grad = jnp.einsum('hqk,khd->qhd', grad_scores_w, keys_wide) * score_scale
        key_acc = key_acc + jnp.einsum('hqk,qhd->khd', grad_scores_w, query_wide) * score_scale
        return ((key_acc, value_acc), query_grad)
    zero_heads = jnp.zeros((length, heads, head_size), jnp.float32)
    pieces = (queries_b.reshape(block_count, block_rows, heads, head_size), grad_mixed_b.reshape(block_count, block_rows, heads, head_size), delta.reshape(block_count, block_rows, heads), log_total, doc_blocks)
    (key_grad, value_grad), query_grad = lax.scan(backward_block, (zero_heads, zero_heads), pieces)
    query_grad = query_grad.reshape(length, heads, head_size)
    grad_qkv_in = jnp.concatenate([rotate_back(query_grad, cosine, sine).reshape(length, width), rotate_back(key_grad, cosine, sine).reshape(length, width), value_grad.reshape(length, width)], axis=1).astype(jnp.bfloat16)
    grad_qkv = contract_rows(act_one, grad_qkv_in)
    grad_act_one = contract_cols(grad_qkv_in, w_qkv_b)
    gain_grad_one = lax.optimization_barrier(jnp.sum(grad_act_one * hat_one, axis=0))
    grad_input = grad_hidden + normalize_back(grad_act_one * gain_one, hat_one, factor_one)
    gain_grads = jnp.stack([gain_grad_one, gain_grad_two])
    return (output.astype(jnp.bfloat16), grad_input, (grad_qkv, grad_out, grad_in, grad_mlp, gain_grads))

def orthogonalize(moment):
    highest = lax.Precision.HIGHEST
    gram_matrix = jnp.dot(moment, moment.T, precision=highest)
    inverse = 1.0 / (jnp.sqrt(jnp.trace(gram_matrix)) + ortho_eps)
    iterate = moment * inverse
    gram_matrix = gram_matrix * (inverse * inverse)
    for sweep_index in range(NS_ITERS):
        first_product = jnp.dot(gram_matrix, iterate, precision=highest)
        second_product = jnp.dot(gram_matrix, first_product, precision=highest)
        iterate = quintic_one * iterate + quintic_two * first_product + quintic_three * second_product
        if sweep_index + 1 < NS_ITERS:
            gram_matrix = jnp.dot(iterate, iterate.T, precision=highest)
    return iterate

def reference(block_input, out_grad, positions, w_qkv, w_attn_out, w_in, w_mlp_out, norm_gains, m_qkv, m_attn_out, m_in, m_mlp_out, gain_mean, gain_var):
    matrices = (w_qkv, w_attn_out, w_in, w_mlp_out)
    moments = (m_qkv, m_attn_out, m_in, m_mlp_out)
    params = tuple((weight.astype(jnp.bfloat16) for weight in matrices)) + (norm_gains.astype(jnp.bfloat16),)

    def sequence_step(carry, pieces):
        x_seq, dy_seq, pos_seq = pieces
        output, grad_input, grads = sequence_pass(params, x_seq, dy_seq, pos_seq)
        return (tuple((total + grad for total, grad in zip(carry, grads))), (output, grad_input))
    zero_grads = tuple((jnp.zeros(weight.shape, jnp.float32) for weight in matrices)) + (jnp.zeros(norm_gains.shape, jnp.float32),)
    totals, (block_output, input_grad) = lax.scan(sequence_step, zero_grads, (block_input, out_grad, positions))
    factor = 1.0 / math.sqrt(TOKENS)
    grads = [total * factor for total in totals]
    new_weights = []
    new_moments = []
    for weight, moment, grad in zip(matrices, moments, grads[:4]):
        moment_next = momentum_rate * moment + grad
        update = orthogonalize(moment_next)
        rate = matrix_rate * math.sqrt(max(weight.shape))
        new_weights.append(weight - rate * update)
        new_moments.append(moment_next)
    gain_grad = grads[4]
    mean_next = beta_first * gain_mean + (1.0 - beta_first) * gain_grad
    var_next = beta_second * gain_var + (1.0 - beta_second) * gain_grad * gain_grad
    gains_next = norm_gains - gain_rate * (mean_next / first_fix) / (jnp.sqrt(var_next / second_fix) + adam_eps)
    return (block_output, input_grad, grads[0], grads[1], grads[2], grads[3], gain_grad, new_weights[0], new_weights[1], new_weights[2], new_weights[3], gains_next, new_moments[0], new_moments[1], new_moments[2], new_moments[3], mean_next, var_next)
```

```python
import functools
import math

import jax
import jax.numpy as jnp
from jax import lax
from jax.experimental import pallas as pl
from jax.experimental.pallas import tpu as pltpu
from jax.sharding import PartitionSpec as P

HEADS = 12
NS_ITERS = 5


theta_base = 160000.0
norm_eps = 1e-05
quintic_one = 3.4445
quintic_two = -4.775
quintic_three = 2.0315
momentum_rate = 0.95
matrix_rate = 0.04
gain_rate = 0.1
beta_first = 0.9
beta_second = 0.95
adam_eps = 1e-08
first_fix = 1.0 - 0.9**10
second_fix = 1.0 - 0.95**10
ortho_eps = 1e-07


def shortened(value):
    return jax.tree.map(lambda a: a.astype(jnp.bfloat16) if a.dtype == jnp.float32 else a, value)


def rope_tables(positions, head_size):
    half_size = head_size // 2
    indices = jnp.arange(half_size, dtype=jnp.float32)
    frequency = jnp.exp(indices * (-2.0 * math.log(theta_base) / head_size))
    angles = positions.astype(jnp.float32)[:, None] * frequency[None, :]
    return (jnp.cos(angles)[:, None, :], jnp.sin(angles)[:, None, :])


def rotate(field, cosine, sine):
    half_size = field.shape[-1] // 2
    first_half = field[..., :half_size]
    second_half = field[..., half_size:]
    return jnp.concatenate(
        [first_half * cosine - second_half * sine, second_half * cosine + first_half * sine],
        axis=-1,
    )


def rotate_back(gradient, cosine, sine):
    half_size = gradient.shape[-1] // 2
    first_half = gradient[..., :half_size]
    second_half = gradient[..., half_size:]
    return jnp.concatenate(
        [first_half * cosine + second_half * sine, second_half * cosine - first_half * sine],
        axis=-1,
    )


def normalize(field):
    centered = field - jnp.mean(field, axis=-1, keepdims=True)
    factor = lax.rsqrt(jnp.mean(centered * centered, axis=-1, keepdims=True) + norm_eps)
    return (centered * factor, factor)


def normalize_back(grad_hat, normed, factor):
    first_mean = jnp.mean(grad_hat, axis=-1, keepdims=True)
    second_mean = jnp.mean(grad_hat * normed, axis=-1, keepdims=True)
    return factor * (grad_hat - first_mean - normed * second_mean)


def gelu_parts(preact):
    cumulative = 0.5 * (1.0 + lax.erf(preact * (1.0 / math.sqrt(2.0))))
    activated = preact * cumulative
    derivative = cumulative + preact * jnp.exp(-0.5 * preact * preact) * (
        1.0 / math.sqrt(2.0 * math.pi)
    )
    return (activated, derivative)


def contract_rows(left_side, right_side):
    return lax.dot_general(
        left_side, right_side, (((0,), (0,)), ((), ())), preferred_element_type=jnp.float32
    )


def contract_cols(left_side, right_side):
    return lax.dot_general(
        left_side, right_side, (((1,), (1,)), ((), ())), preferred_element_type=jnp.float32
    )


def pair_terms(
    query_heads,
    grad_heads,
    delta_rows,
    log_rows,
    query_docs,
    key_heads,
    value_heads,
    key_docs,
    score_scale,
):
    f32 = jnp.float32
    scores = (
        jnp.einsum("qhd,khd->hqk", query_heads, key_heads, preferred_element_type=f32) * score_scale
    )
    same = (query_docs[:, None] == key_docs[None, :])[None]
    probs = jnp.where(same, jnp.exp(scores - log_rows[:, :, None]), 0.0)
    grad_probs = jnp.einsum("qhd,khd->hqk", grad_heads, value_heads, preferred_element_type=f32)
    grad_scores_b = (probs * (grad_probs - jnp.transpose(delta_rows)[:, :, None])).astype(
        jnp.bfloat16
    )
    return (probs.astype(jnp.bfloat16), grad_scores_b)


def gram_of(iterate):
    highest = lax.Precision.HIGHEST
    owned_rows = iterate.shape[0] // lax.axis_size("ctx")
    picked = lax.slice_in_dim(iterate, 0, owned_rows * lax.axis_size("ctx"), axis=0)
    gram_share = lax.psum_scatter(
        jnp.dot(picked, iterate.T, precision=highest, preferred_element_type=jnp.float32).astype(
            jnp.bfloat16
        ),
        "ctx",
        scatter_dimension=0,
        tiled=True,
    ).astype(jnp.float32)
    return lax.all_gather(gram_share.astype(jnp.bfloat16), "ctx", axis=0, tiled=True).astype(
        gram_share.dtype
    )


def orthogonalize(moment):
    highest = lax.Precision.HIGHEST
    gram_matrix = gram_of(moment)
    inverse = 1.0 / (jnp.sqrt(jnp.trace(gram_matrix)) + ortho_eps)
    iterate = moment * inverse
    gram_matrix = gram_matrix * (inverse * inverse)
    for sweep_index in range(NS_ITERS):
        first_product = jnp.dot(gram_matrix, iterate, precision=highest)
        second_product = jnp.dot(gram_matrix, first_product, precision=highest)
        iterate = (
            quintic_one * iterate + quintic_two * first_product + quintic_three * second_product
        )
        if sweep_index + 1 < NS_ITERS:
            gram_matrix = gram_of(iterate)
    return iterate


def per_device(
    block_input,
    out_grad,
    positions,
    w_qkv,
    w_attn_out,
    w_in,
    w_mlp_out,
    norm_gains,
    m_qkv,
    m_attn_out,
    m_in,
    m_mlp_out,
    gain_mean,
    gain_var,
):
    bf16 = jnp.bfloat16
    f32 = jnp.float32
    dp_count = lax.axis_size("dp")
    ctx_count = lax.axis_size("ctx")
    tok_rows = block_input.shape[1]
    width = block_input.shape[2]
    heads = HEADS
    head_size = width // heads
    score_scale = 1.0 / math.sqrt(head_size)
    seq_length = tok_rows * ctx_count
    key_block = math.gcd(seq_length, 512)
    block_count = seq_length // key_block
    gathered = (
        lax.all_gather(w_qkv.astype(bf16), "dp", axis=0, tiled=True),
        lax.all_gather(w_attn_out.astype(bf16), "dp", axis=0, tiled=True),
        lax.all_gather(w_in.astype(bf16), "dp", axis=0, tiled=True),
        lax.all_gather(w_mlp_out.astype(bf16), "dp", axis=0, tiled=True),
        lax.all_gather(norm_gains.astype(bf16), "dp", axis=1, tiled=True),
    )
    w_qkv_b, w_out_b, w_in_b, w_mlp_b, gains_b = gathered
    gain_one = gains_b[0].astype(f32)
    gain_two = gains_b[1].astype(f32)
    x_wide = block_input[0].astype(f32)
    dy_seq = out_grad[0]
    hat_one, factor_one = normalize(x_wide)
    act_one = (hat_one * gain_one).astype(bf16)
    qkv = jnp.dot(act_one, w_qkv_b, preferred_element_type=f32)
    cosine, sine = rope_tables(positions[0], head_size)
    doc_own = (
        lax.axis_index("ctx") * tok_rows + jnp.arange(tok_rows, dtype=jnp.int32) - positions[0]
    )
    queries_b = rotate(qkv[:, :width].reshape(tok_rows, heads, head_size), cosine, sine).astype(
        bf16
    )
    keys_flat = (
        rotate(qkv[:, width : 2 * width].reshape(tok_rows, heads, head_size), cosine, sine)
        .astype(bf16)
        .reshape(tok_rows, width)
    )
    values_flat = qkv[:, 2 * width :].astype(bf16)
    key_piece = lax.all_gather(keys_flat, "ctx", axis=0, tiled=True)
    value_piece = lax.all_gather(values_flat, "ctx", axis=0, tiled=True)
    doc_piece = lax.all_gather(doc_own, "ctx", axis=0, tiled=True)
    rows_here = key_piece.shape[0]
    key_heads = key_piece.reshape(rows_here, heads, head_size)
    value_heads = value_piece.reshape(rows_here, heads, head_size)
    scores = (
        jnp.einsum("qhd,khd->hqk", queries_b, key_heads, preferred_element_type=f32) * score_scale
    )
    same = (doc_own[:, None] == doc_piece[None, :])[None]
    weights = jnp.where(same, jnp.exp(scores), 0.0)
    totals = jnp.sum(weights, axis=-1)
    summed = jnp.einsum(
        "hqk,khd->qhd", weights.astype(bf16), value_heads, preferred_element_type=f32
    )
    fold_result = (summed, totals)
    summed_values, total_weights = fold_result
    attended = summed_values / jnp.transpose(total_weights)[:, :, None]
    log_total = jnp.log(total_weights)
    mixed_b = attended.reshape(tok_rows, width).astype(bf16)
    hidden = x_wide + jnp.dot(mixed_b, w_out_b, preferred_element_type=f32)
    hat_two, factor_two = normalize(hidden)
    act_two = (hat_two * gain_two).astype(bf16)
    lifted = jnp.dot(act_two, w_in_b, preferred_element_type=f32)
    hidden_units = lifted.shape[1] // 2
    preact = lifted[:, :hidden_units]
    gate_half = lifted[:, hidden_units:]
    activated, derivative = gelu_parts(preact)
    inner_b = (activated * gate_half).astype(bf16)
    output = hidden + contract_cols(inner_b, w_mlp_b)
    dy_wide = dy_seq.astype(f32)
    grad_mlp = contract_rows(dy_seq, inner_b)
    grad_inner = jnp.dot(dy_seq, w_mlp_b, preferred_element_type=f32)
    grad_lift = jnp.concatenate(
        [grad_inner * gate_half * derivative, grad_inner * activated], axis=1
    ).astype(bf16)
    grad_in = contract_rows(act_two, grad_lift)
    grad_act_two = contract_cols(grad_lift, w_in_b)
    gain_grad_two = jnp.sum(grad_act_two * hat_two, axis=0)
    grad_hidden = dy_wide + normalize_back(grad_act_two * gain_two, hat_two, factor_two)
    grad_hidden_b = grad_hidden.astype(bf16)
    grad_out = contract_rows(mixed_b, grad_hidden_b)
    grad_mixed = contract_cols(grad_hidden_b, w_out_b).reshape(tok_rows, heads, head_size)
    delta = jnp.sum(grad_mixed * attended, axis=-1)
    grad_mixed_b = grad_mixed.astype(bf16)
    keys_all, values_all, docs_all = (
        lax.all_gather(keys_flat, "ctx", axis=0, tiled=True),
        lax.all_gather(values_flat, "ctx", axis=0, tiled=True),
        lax.all_gather(doc_own, "ctx", axis=0, tiled=True),
    )
    key_pieces = (
        keys_all.reshape(block_count, key_block, width),
        values_all.reshape(block_count, key_block, width),
        docs_all.reshape(block_count, key_block),
    )
    zero_query = jnp.zeros((tok_rows, heads, head_size), f32)

    def query_only_step(query_grad, pieces):
        key_piece, value_piece, doc_piece = pieces
        key_heads = key_piece.reshape(key_block, heads, head_size)
        value_heads = value_piece.reshape(key_block, heads, head_size)
        probs_b, grad_scores_b = pair_terms(
            queries_b,
            grad_mixed_b,
            delta,
            log_total,
            doc_own,
            key_heads,
            value_heads,
            doc_piece,
            score_scale,
        )
        query_grad = (
            query_grad
            + jnp.einsum("hqk,khd->qhd", grad_scores_b, key_heads, preferred_element_type=f32)
            * score_scale
        )
        return (query_grad, None)

    query_grad, unused_terms = lax.scan(query_only_step, zero_query, key_pieces)
    queries_all, grads_all, logs_all, deltas_all, qdocs_all = (
        lax.all_gather(queries_b.reshape(tok_rows, width), "ctx", axis=0, tiled=True),
        lax.all_gather(grad_mixed_b.reshape(tok_rows, width), "ctx", axis=0, tiled=True),
        lax.all_gather(log_total.astype(jnp.bfloat16), "ctx", axis=1, tiled=True).astype(
            log_total.dtype
        ),
        lax.all_gather(delta.astype(jnp.bfloat16), "ctx", axis=0, tiled=True).astype(delta.dtype),
        lax.all_gather(doc_own, "ctx", axis=0, tiled=True),
    )
    own_keys = keys_flat.reshape(tok_rows, heads, head_size)
    own_values = values_flat.reshape(tok_rows, heads, head_size)

    def key_side_step(carry, pieces):
        key_acc, value_acc = carry
        query_piece, grad_piece, log_piece, delta_piece, qdoc_piece = pieces
        query_heads = query_piece.reshape(key_block, heads, head_size)
        grad_heads = grad_piece.reshape(key_block, heads, head_size)
        probs_b, grad_scores_b = pair_terms(
            query_heads,
            grad_heads,
            delta_piece,
            log_piece,
            qdoc_piece,
            own_keys,
            own_values,
            doc_own,
            score_scale,
        )
        value_acc = value_acc + jnp.einsum(
            "hqk,qhd->khd", probs_b, grad_heads, preferred_element_type=f32
        )
        key_acc = (
            key_acc
            + jnp.einsum("hqk,qhd->khd", grad_scores_b, query_heads, preferred_element_type=f32)
            * score_scale
        )
        return ((key_acc, value_acc), None)

    query_pieces = (
        queries_all.reshape(block_count, key_block, width),
        grads_all.reshape(block_count, key_block, width),
        jnp.transpose(logs_all.reshape(heads, block_count, key_block), (1, 0, 2)),
        deltas_all.reshape(block_count, key_block, heads),
        qdocs_all.reshape(block_count, key_block),
    )
    (key_acc, value_acc), unused_side = lax.scan(
        key_side_step, (zero_query, zero_query), query_pieces
    )
    key_grad = key_acc.reshape(tok_rows, width)
    value_grad = value_acc.reshape(tok_rows, width)
    grad_qkv_in = jnp.concatenate(
        [
            rotate_back(query_grad, cosine, sine).reshape(tok_rows, width),
            rotate_back(key_grad.reshape(tok_rows, heads, head_size), cosine, sine).reshape(
                tok_rows, width
            ),
            value_grad,
        ],
        axis=1,
    ).astype(bf16)
    grad_qkv = contract_rows(act_one, grad_qkv_in)
    grad_act_one = contract_cols(grad_qkv_in, w_qkv_b)
    gain_grad_one = jnp.sum(grad_act_one * hat_one, axis=0)
    grad_input = grad_hidden + normalize_back(grad_act_one * gain_one, hat_one, factor_one)
    gain_grads = jnp.stack([gain_grad_one, gain_grad_two])
    shares = (
        lax.psum_scatter(
            grad_qkv.astype(jnp.bfloat16), "dp", scatter_dimension=0, tiled=True
        ).astype(jnp.float32),
        lax.psum_scatter(
            grad_out.astype(jnp.bfloat16), "dp", scatter_dimension=0, tiled=True
        ).astype(jnp.float32),
        lax.psum_scatter(
            grad_in.astype(jnp.bfloat16), "dp", scatter_dimension=0, tiled=True
        ).astype(jnp.float32),
        lax.psum_scatter(
            grad_mlp.astype(jnp.bfloat16), "dp", scatter_dimension=0, tiled=True
        ).astype(jnp.float32),
        lax.psum_scatter(
            gain_grads.astype(jnp.bfloat16), "dp", scatter_dimension=1, tiled=True
        ).astype(jnp.float32),
    )
    summed_grads = (
        lax.psum(shares[0].astype(jnp.bfloat16), "ctx").astype(jnp.float32),
        lax.psum(shares[1].astype(jnp.bfloat16), "ctx").astype(jnp.float32),
        lax.psum(shares[2].astype(jnp.bfloat16), "ctx").astype(jnp.float32),
        lax.psum(shares[3].astype(jnp.bfloat16), "ctx").astype(jnp.float32),
        lax.psum(shares[4].astype(jnp.bfloat16), "ctx").astype(jnp.float32),
    )
    factor = 1.0 / math.sqrt(dp_count * ctx_count * tok_rows)
    grads = [total * factor for total in summed_grads]
    matrices = (w_qkv, w_attn_out, w_in, w_mlp_out)
    moments = (m_qkv, m_attn_out, m_in, m_mlp_out)
    moments_next = [momentum_rate * moment + grad for moment, grad in zip(moments, grads[:4])]
    owned_rows = w_qkv.shape[0]
    widest = max(w_qkv.shape[1], w_in.shape[1])
    col_count = widest // ctx_count
    ctx_place = lax.axis_index("ctx")

    def owner_slice(matrix):
        padded = jnp.pad(matrix, ((0, 0), (0, widest - matrix.shape[1])))
        return lax.dynamic_slice_in_dim(padded, ctx_place * col_count, col_count, 1)

    filled_slots = jnp.stack([owner_slice(moment) for moment in moments_next])
    empty_slots = jnp.zeros((dp_count - 4, owned_rows, col_count), f32)
    send_buffer = jnp.concatenate([filled_slots, empty_slots], axis=0)
    received = lax.all_to_all(
        send_buffer.astype(jnp.bfloat16), "dp", split_axis=0, concat_axis=0, tiled=True
    ).astype(send_buffer.dtype)
    owned_matrix = received.reshape(dp_count * owned_rows, col_count)
    orthogonal = orthogonalize(owned_matrix)
    returned = lax.all_to_all(
        shortened(orthogonal.reshape(dp_count, owned_rows, col_count)),
        "dp",
        split_axis=0,
        concat_axis=0,
        tiled=True,
    )
    updates = lax.all_gather(shortened(returned[:4]), "ctx", axis=2, tiled=True)
    new_weights = []
    for slot_index in range(4):
        weight = matrices[slot_index]
        full_rows = weight.shape[0] * dp_count
        rate = matrix_rate * math.sqrt(max(full_rows, weight.shape[1]))
        new_weights.append(weight - rate * updates[slot_index][:, : weight.shape[1]])
    gain_grad = grads[4]
    mean_next = beta_first * gain_mean + (1.0 - beta_first) * gain_grad
    var_next = beta_second * gain_var + (1.0 - beta_second) * gain_grad * gain_grad
    gains_next = norm_gains - gain_rate * (mean_next / first_fix) / (
        jnp.sqrt(var_next / second_fix) + adam_eps
    )
    return (
        output.astype(bf16)[None],
        grad_input[None],
        grads[0],
        grads[1],
        grads[2],
        grads[3],
        gain_grad,
        new_weights[0],
        new_weights[1],
        new_weights[2],
        new_weights[3],
        gains_next,
        moments_next[0],
        moments_next[1],
        moments_next[2],
        moments_next[3],
        mean_next,
        var_next,
    )


def ring_places(mesh):
    chip_count = mesh.shape["dp"] // 2
    natural = list(range(chip_count))
    try:
        column = [mesh.devices[2 * chip, 0] for chip in natural]
        partner = [mesh.devices[2 * chip + 1, 0] for chip in natural]
        coords = [tuple(device.coords) for device in column]
        if coords != [tuple(device.coords) for device in partner]:
            return natural
    except (AttributeError, IndexError):
        return natural
    dims = [dim for dim in range(3) if len({c[dim] for c in coords}) > 1]
    narrow = [dim for dim in dims if len({c[dim] for c in coords}) == 2]
    if len(dims) != 2 or not narrow:
        return natural
    split = narrow[0]
    along = [dim for dim in dims if dim != split][0]
    low = min(c[split] for c in coords)
    first = sorted((c for c in natural if coords[c][split] == low), key=lambda c: coords[c][along])
    second = sorted((c for c in natural if coords[c][split] != low), key=lambda c: -coords[c][along])
    return first + second


def place_rows(pieces, indices, widths):
    count = len(pieces)
    rows = pieces[0].shape[0]
    offsets = [sum(widths[:k]) for k in range(len(widths))]

    def body(*refs):
        index_ref = refs[0]
        piece_refs = refs[1 : 1 + count]
        out_refs = refs[1 + count : 1 + count + len(widths)]
        sems = refs[-1]
        copies = []
        for piece_at in range(count):
            start = pl.multiple_of(index_ref[piece_at] * rows, rows)
            for width_at, width in enumerate(widths):
                source = piece_refs[piece_at].at[:, pl.ds(offsets[width_at], width)]
                target = out_refs[width_at].at[pl.ds(start, rows), :]
                copies.append(
                    pltpu.make_async_copy(source, target, sems.at[piece_at, width_at])
                )
        for copy in copies:
            copy.start()
        for copy in copies:
            copy.wait()

    anywhere = pl.BlockSpec(memory_space=pl.ANY)
    return pl.pallas_call(
        body,
        in_specs=[pl.BlockSpec(memory_space=pltpu.SMEM)] + [anywhere] * count,
        out_specs=[anywhere] * len(widths),
        out_shape=[
            jax.ShapeDtypeStruct((count * rows, width), pieces[0].dtype) for width in widths
        ],
        scratch_shapes=[pltpu.SemaphoreType.DMA((count, len(widths)))],
    )(indices, *pieces)


def sweep_rows(start_rows, picked_rows):
    high = lax.Precision.HIGH
    f32 = jnp.float32
    gram = contract_cols(start_rows, start_rows)
    inverse = 1.0 / (jnp.sqrt(jnp.trace(gram)) + ortho_eps)
    gram = gram * (inverse * inverse)
    identity = jnp.eye(gram.shape[0], dtype=f32)
    top = None
    for sweep_index in range(NS_ITERS):
        last = sweep_index + 1 == NS_ITERS
        if last and top is not None:
            inner = quintic_two * top + quintic_three * jnp.dot(top, gram, precision=high)
            top = quintic_one * top + jnp.dot(inner, gram, precision=high)
            break
        square = jnp.dot(gram, gram, precision=high)
        factor = quintic_one * identity + quintic_two * gram + quintic_three * square
        if top is None:
            top = factor[:picked_rows]
        else:
            top = jnp.dot(top, factor, precision=high)
        if not last:
            gram = jnp.dot(jnp.dot(gram, factor, precision=high), factor, precision=high)
    return jnp.dot((top * inverse).astype(jnp.bfloat16), start_rows, preferred_element_type=f32)


def paired_device(order, *arrays):
    (
        block_input,
        out_grad,
        positions,
        w_qkv,
        w_attn_out,
        w_in,
        w_mlp_out,
        norm_gains,
        m_qkv,
        m_attn_out,
        m_in,
        m_mlp_out,
        gain_mean,
        gain_var,
    ) = arrays
    bf16 = jnp.bfloat16
    f32 = jnp.float32
    dp_count = lax.axis_size("dp")
    ctx_count = lax.axis_size("ctx")
    chip_count = dp_count // 2
    dp_at = lax.axis_index("dp")
    half_at = lax.axis_index("ctx")
    low_half = half_at == 0
    core_at = dp_at % 2
    tok_rows = block_input.shape[1]
    width = block_input.shape[2]
    length = tok_rows * ctx_count
    heads = HEADS // ctx_count
    head_size = width // HEADS
    span = heads * head_size
    score_scale = 1.0 / math.sqrt(head_size)
    owned_rows = w_qkv.shape[0]
    hidden_units = w_mlp_out.shape[1]
    hidden_half = hidden_units // 2
    place = [0] * chip_count
    for spot, chip in enumerate(order):
        place[chip] = spot
    order_table = jnp.array(order, jnp.int32)
    spot_at = jnp.array(place, jnp.int32)[dp_at // 2]

    def ring_pairs(step):
        return [
            (2 * order[spot] + core, 2 * order[(spot + step) % chip_count] + core)
            for spot in range(chip_count)
            for core in range(2)
        ]

    forward_pairs = ring_pairs(1)
    backward_pairs = ring_pairs(-1)
    core_pairs = [(index, index ^ 1) for index in range(dp_count)]
    flip_pairs = [(0, 1), (1, 0)]

    def chip_index(step):
        return order_table[(spot_at + step + chip_count) % chip_count]

    def swap_core(value):
        return lax.ppermute(value, "dp", core_pairs)

    def swap_half(value):
        return lax.ppermute(value, "ctx", flip_pairs)

    ahead_steps = chip_count // 2
    behind_steps = chip_count - 1 - ahead_steps

    def ring_collect(shard):
        steps = [0]
        pieces = [shard]
        ahead = shard
        behind = shard
        for step in range(1, ahead_steps + 1):
            ahead = lax.ppermute(ahead, "dp", forward_pairs)
            steps.append(-step)
            pieces.append(ahead)
            if step <= behind_steps:
                behind = lax.ppermute(behind, "dp", backward_pairs)
                steps.append(step)
                pieces.append(behind)
        return steps, pieces

    def collect(shard, widths):
        steps, pieces = ring_collect(shard)
        others = [swap_core(piece) for piece in pieces]
        chips = jnp.stack([chip_index(step) for step in steps])
        indices = jnp.concatenate([2 * chips + core_at, 2 * chips + 1 - core_at])
        return place_rows(pieces + others, indices, widths)

    def ring_reduce(partial):
        columns = partial.shape[1]
        split = partial.reshape(chip_count, 2, owned_rows, columns)
        even, odd = split[:, 0], split[:, 1]
        is_even = core_at == 0
        kept = jnp.where(is_even, even, odd)
        given = jnp.where(is_even, odd, even)
        chunks = (kept.astype(f32) + swap_core(given).astype(f32)).astype(bf16)

        def chunk(step):
            return lax.dynamic_index_in_dim(chunks, chip_index(step), 0, keepdims=False)

        ahead = chunk(ahead_steps)
        behind = chunk(-behind_steps)
        for step in range(ahead_steps, 0, -1):
            ahead = lax.ppermute(ahead, "dp", forward_pairs)
            if step > 1:
                ahead = (ahead.astype(f32) + chunk(step - 1).astype(f32)).astype(bf16)
            if step <= behind_steps:
                behind = lax.ppermute(behind, "dp", backward_pairs)
                if step > 1:
                    behind = (behind.astype(f32) + chunk(1 - step).astype(f32)).astype(bf16)
        return (chunk(0).astype(f32) + ahead.astype(f32) + behind.astype(f32)).astype(bf16)

    def my_half(matrix, parts):
        rows = matrix.shape[0]
        split = matrix.reshape(rows, parts, 2, -1)
        picked = jnp.where(low_half, split[:, :, 0], split[:, :, 1])
        return picked.reshape(rows, -1)

    def ordered(own, other, axis):
        first = jnp.where(low_half, own, other)
        second = jnp.where(low_half, other, own)
        return jnp.concatenate([first, second], axis=axis)

    gain_columns = jnp.pad(jnp.transpose(norm_gains), ((0, 0), (0, 128 - norm_gains.shape[0])))
    first_shard = jnp.concatenate([my_half(w_qkv, 3), gain_columns], axis=1).astype(bf16)
    pad_units = -hidden_half % 128
    second_shard = jnp.concatenate(
        [
            w_attn_out,
            my_half(w_in, 2),
            jnp.pad(my_half(w_mlp_out, 1), ((0, 0), (0, pad_units))),
        ],
        axis=1,
    ).astype(bf16)

    own_places = positions[0]
    digits = jnp.stack([own_places // 128, own_places % 128]).astype(bf16)
    digit_rows = jnp.pad(digits, ((0, 14), (0, width - tok_rows)))
    own_pack = jnp.concatenate([block_input[0], out_grad[0], digit_rows], axis=0)
    other_pack = swap_half(own_pack)
    w_qkv_h, gains_t = collect(first_shard, (3 * span, 128))
    w_out_b, w_in_h, w_mlp_p = collect(
        second_shard, (width, 2 * hidden_half, hidden_half + pad_units)
    )
    w_mlp_h = w_mlp_p[:, :hidden_half]

    other_digits = other_pack[2 * tok_rows : 2 * tok_rows + 2, :tok_rows].astype(jnp.int32)
    other_places = other_digits[0] * 128 + other_digits[1]
    places = ordered(own_places, other_places, 0)
    x_wide = ordered(own_pack[:tok_rows], other_pack[:tok_rows], 0).astype(f32)
    dy_b = ordered(own_pack[tok_rows : 2 * tok_rows], other_pack[tok_rows : 2 * tok_rows], 0)
    cosine, sine = rope_tables(places, head_size)
    starts = jnp.arange(length, dtype=jnp.int32) - places
    same = (starts[:, None] == starts[None, :])[None]
    gains_w = gains_t[:, :2].astype(f32)
    gain_one = gains_w[:, 0]
    gain_two = gains_w[:, 1]

    hat_one, factor_one = normalize(x_wide)
    act_one = (hat_one * gain_one).astype(bf16)
    qkv = jnp.dot(act_one, w_qkv_h, preferred_element_type=f32)
    queries_b = rotate(qkv[:, :span].reshape(length, heads, head_size), cosine, sine).astype(bf16)
    keys_b = rotate(qkv[:, span : 2 * span].reshape(length, heads, head_size), cosine, sine).astype(
        bf16
    )
    values_b = qkv[:, 2 * span :].astype(bf16).reshape(length, heads, head_size)
    scores = (
        jnp.einsum("qhd,khd->hqk", queries_b, keys_b, preferred_element_type=f32) * score_scale
    )
    weights = jnp.where(same, jnp.exp(scores), 0.0)
    totals = jnp.sum(weights, axis=-1)
    summed = jnp.einsum("hqk,khd->qhd", weights.astype(bf16), values_b, preferred_element_type=f32)
    attended = summed / jnp.transpose(totals)[:, :, None]
    log_total = jnp.log(totals)
    own_mixed = attended.reshape(length, span).astype(bf16)
    mixed_b = ordered(own_mixed, swap_half(own_mixed), 1)

    hidden = x_wide + jnp.dot(mixed_b, w_out_b, preferred_element_type=f32)
    hat_two, factor_two = normalize(hidden)
    act_two = (hat_two * gain_two).astype(bf16)
    lifted = jnp.dot(act_two, w_in_h, preferred_element_type=f32)
    preact = lifted[:, :hidden_half]
    gate_half = lifted[:, hidden_half:]
    activated, derivative = gelu_parts(preact)
    inner_b = (activated * gate_half).astype(bf16)
    grad_inner = jnp.dot(dy_b, w_mlp_h, preferred_element_type=f32)
    grad_lift = jnp.concatenate(
        [grad_inner * gate_half * derivative, grad_inner * activated], axis=1
    ).astype(bf16)
    grad_two_part = contract_cols(grad_lift, w_in_h)
    grad_act_two = grad_two_part + swap_half(grad_two_part.astype(bf16)).astype(f32)

    def own_tokens(field):
        return jnp.where(low_half, field[:tok_rows], field[tok_rows:])

    def other_tokens(field):
        return jnp.where(low_half, field[tok_rows:], field[:tok_rows])

    out_part = contract_cols(inner_b, w_mlp_h)
    output = (
        own_tokens(hidden)
        + own_tokens(out_part)
        + swap_half(other_tokens(out_part).astype(bf16)).astype(f32)
    )
    grad_mlp = contract_rows(dy_b, inner_b)
    grad_in = contract_rows(act_two, grad_lift)
    early_rows = ring_reduce(jnp.concatenate([grad_in, grad_mlp], axis=1).astype(bf16))

    gain_grad_two = jnp.sum(grad_two_part * hat_two, axis=0)
    grad_hidden = dy_b.astype(f32) + normalize_back(grad_act_two * gain_two, hat_two, factor_two)
    grad_hidden_b = grad_hidden.astype(bf16)
    grad_out = contract_rows(
        mixed_b, jnp.where(low_half, grad_hidden_b[:, :span], grad_hidden_b[:, span:])
    )
    out_rows_h = jnp.where(low_half, w_out_b[:span], w_out_b[span:])
    grad_mixed = contract_cols(grad_hidden_b, out_rows_h).reshape(length, heads, head_size)
    delta = jnp.sum(grad_mixed * attended, axis=-1)
    grad_mixed_b = grad_mixed.astype(bf16)
    probs = jnp.where(same, jnp.exp(scores - log_total[:, :, None]), 0.0)
    grad_probs = jnp.einsum("qhd,khd->hqk", grad_mixed_b, values_b, preferred_element_type=f32)
    grad_scores_b = (probs * (grad_probs - jnp.transpose(delta)[:, :, None])).astype(bf16)
    query_grad = (
        jnp.einsum("hqk,khd->qhd", grad_scores_b, keys_b, preferred_element_type=f32) * score_scale
    )
    key_grad = (
        jnp.einsum("hqk,qhd->khd", grad_scores_b, queries_b, preferred_element_type=f32)
        * score_scale
    )
    value_grad = jnp.einsum(
        "hqk,qhd->khd", probs.astype(bf16), grad_mixed_b, preferred_element_type=f32
    )
    grad_qkv_in = jnp.concatenate(
        [
            rotate_back(query_grad, cosine, sine).reshape(length, span),
            rotate_back(key_grad, cosine, sine).reshape(length, span),
            value_grad.reshape(length, span),
        ],
        axis=1,
    ).astype(bf16)
    grad_qkv = contract_rows(act_one, grad_qkv_in)
    grad_one_part = contract_cols(grad_qkv_in, w_qkv_h)
    gain_grad_one = jnp.sum(grad_one_part * hat_one, axis=0)
    gain_pair = jnp.pad(jnp.stack([gain_grad_one, gain_grad_two], axis=1), ((0, 0), (0, 126)))
    late_rows = ring_reduce(jnp.concatenate([grad_qkv, grad_out, gain_pair], axis=1).astype(bf16))

    grad_act_one = own_tokens(grad_one_part) + swap_half(
        other_tokens(grad_one_part).astype(bf16)
    ).astype(f32)
    grad_input = own_tokens(grad_hidden) + normalize_back(
        grad_act_one * gain_one, own_tokens(hat_one), own_tokens(factor_one)
    )

    def whole_columns(own, other, parts):
        rows = own.shape[0]
        first = jnp.where(low_half, own, other).reshape(rows, parts, -1)
        second = jnp.where(low_half, other, own).reshape(rows, parts, -1)
        return jnp.stack([first, second], axis=2).reshape(rows, -1).astype(f32)

    factor = 1.0 / math.sqrt(dp_count * length)
    early_other = swap_half(early_rows)
    late_other = swap_half(late_rows)
    cut = 2 * hidden_half
    grads = [
        whole_columns(late_rows[:, : 3 * span], late_other[:, : 3 * span], 3) * factor,
        whole_columns(
            late_rows[:, 3 * span : 3 * span + span], late_other[:, 3 * span : 3 * span + span], 1
        )
        * factor,
        whole_columns(early_rows[:, :cut], early_other[:, :cut], 2) * factor,
        whole_columns(early_rows[:, cut:], early_other[:, cut:], 1) * factor,
    ]
    gain_sum = late_rows[:, 4 * span :].astype(f32) + late_other[:, 4 * span :].astype(f32)
    gain_grad = jnp.transpose(gain_sum)[:2] * factor

    matrices = (w_qkv, w_attn_out, w_in, w_mlp_out)
    moments = (m_qkv, m_attn_out, m_in, m_mlp_out)
    moments_next = [momentum_rate * moment + grad for moment, grad in zip(moments, grads)]
    widest = max(moment.shape[1] for moment in moments)
    slots = jnp.stack(
        [
            jnp.pad(moment.astype(bf16), ((0, 0), (0, widest - moment.shape[1])))
            for moment in moments_next
        ]
    )
    group = dp_count // 4
    group_at = dp_at // group

    def shift_pairs(step):
        return [(index, (index + step * group) % dp_count) for index in range(dp_count)]

    blocks = [lax.dynamic_index_in_dim(slots, group_at, 0, keepdims=False)]
    for step in range(1, 4):
        given = lax.dynamic_index_in_dim(slots, (group_at + step) % 4, 0, keepdims=False)
        blocks.append(lax.ppermute(given, "dp", shift_pairs(step)))
    held = jnp.concatenate(blocks, axis=0)
    reach = 2
    while reach < group:
        pairs = [(index, index ^ reach) for index in range(dp_count)]
        held = jnp.concatenate([held, lax.ppermute(held, "dp", pairs)], axis=0)
        reach *= 2
    held = jnp.concatenate([held, swap_core(held)], axis=0)
    turned = sweep_rows(held, 4 * owned_rows).astype(bf16).reshape(4, owned_rows, widest)
    returned = [turned[0]]
    for step in range(1, 4):
        returned.append(lax.ppermute(turned[step], "dp", shift_pairs(-step)))
    updates = jnp.stack(returned)
    new_weights = []
    for slot_index, weight in enumerate(matrices):
        update = lax.dynamic_index_in_dim(updates, (slot_index - group_at + 4) % 4, 0, False)
        rate = matrix_rate * math.sqrt(max(weight.shape[0] * dp_count, weight.shape[1]))
        new_weights.append(weight - rate * update[:, : weight.shape[1]].astype(f32))
    mean_next = beta_first * gain_mean + (1.0 - beta_first) * gain_grad
    var_next = beta_second * gain_var + (1.0 - beta_second) * gain_grad * gain_grad
    gains_next = norm_gains - gain_rate * (mean_next / first_fix) / (
        jnp.sqrt(var_next / second_fix) + adam_eps
    )
    return (
        output.astype(bf16)[None],
        grad_input[None],
        *grads,
        gain_grad,
        *new_weights,
        gains_next,
        *moments_next,
        mean_next,
        var_next,
    )


def fits_pairs(mesh):
    dp_count, ctx_count = mesh.shape["dp"], mesh.shape["ctx"]
    return ctx_count == 2 and HEADS % 2 == 0 and dp_count % 8 == 0


def solution(mesh):
    placed = (
        P("dp", "ctx", None),
        P("dp", "ctx", None),
        P("dp", "ctx"),
        P("dp", None),
        P("dp", None),
        P("dp", None),
        P("dp", None),
        P(None, "dp"),
        P("dp", None),
        P("dp", None),
        P("dp", None),
        P("dp", None),
        P(None, "dp"),
        P(None, "dp"),
    )
    body = per_device
    if fits_pairs(mesh):
        body = functools.partial(paired_device, ring_places(mesh))
    return jax.shard_map(
        body,
        mesh=mesh,
        in_specs=placed,
        out_specs=(
            P("dp", "ctx", None),
            P("dp", "ctx", None),
            P("dp", None),
            P("dp", None),
            P("dp", None),
            P("dp", None),
            P(None, "dp"),
            P("dp", None),
            P("dp", None),
            P("dp", None),
            P("dp", None),
            P(None, "dp"),
            P("dp", None),
            P("dp", None),
            P("dp", None),
            P("dp", None),
            P(None, "dp"),
            P(None, "dp"),
        ),
        check_vma=False,
    )
```

```python
import functools
import math

import jax
import jax.numpy as jnp
from jax import lax
from jax.experimental import pallas as pl
from jax.experimental.pallas import tpu as pltpu
from jax.sharding import PartitionSpec as P

HEADS = 12
NS_ITERS = 5


theta_base = 160000.0
norm_eps = 1e-05
quintic_one = 3.4445
quintic_two = -4.775
quintic_three = 2.0315
momentum_rate = 0.95
matrix_rate = 0.04
gain_rate = 0.1
beta_first = 0.9
beta_second = 0.95
adam_eps = 1e-08
first_fix = 1.0 - 0.9**10
second_fix = 1.0 - 0.95**10
ortho_eps = 1e-07


def shortened(value):
    return jax.tree.map(lambda a: a.astype(jnp.bfloat16) if a.dtype == jnp.float32 else a, value)


def rope_tables(positions, head_size):
    half_size = head_size // 2
    indices = jnp.arange(half_size, dtype=jnp.float32)
    frequency = jnp.exp(indices * (-2.0 * math.log(theta_base) / head_size))
    angles = positions.astype(jnp.float32)[:, None] * frequency[None, :]
    return (jnp.cos(angles)[:, None, :], jnp.sin(angles)[:, None, :])


def rotate(field, cosine, sine):
    half_size = field.shape[-1] // 2
    first_half = field[..., :half_size]
    second_half = field[..., half_size:]
    return jnp.concatenate(
        [first_half * cosine - second_half * sine, second_half * cosine + first_half * sine],
        axis=-1,
    )


def rotate_back(gradient, cosine, sine):
    half_size = gradient.shape[-1] // 2
    first_half = gradient[..., :half_size]
    second_half = gradient[..., half_size:]
    return jnp.concatenate(
        [first_half * cosine + second_half * sine, second_half * cosine - first_half * sine],
        axis=-1,
    )


def normalize(field):
    centered = field - jnp.mean(field, axis=-1, keepdims=True)
    factor = lax.rsqrt(jnp.mean(centered * centered, axis=-1, keepdims=True) + norm_eps)
    return (centered * factor, factor)


def normalize_back(grad_hat, normed, factor):
    first_mean = jnp.mean(grad_hat, axis=-1, keepdims=True)
    second_mean = jnp.mean(grad_hat * normed, axis=-1, keepdims=True)
    return factor * (grad_hat - first_mean - normed * second_mean)


def gelu_parts(preact):
    cumulative = 0.5 * (1.0 + lax.erf(preact * (1.0 / math.sqrt(2.0))))
    activated = preact * cumulative
    derivative = cumulative + preact * jnp.exp(-0.5 * preact * preact) * (
        1.0 / math.sqrt(2.0 * math.pi)
    )
    return (activated, derivative)


def contract_rows(left_side, right_side):
    return lax.dot_general(
        left_side, right_side, (((0,), (0,)), ((), ())), preferred_element_type=jnp.float32
    )


def contract_cols(left_side, right_side):
    return lax.dot_general(
        left_side, right_side, (((1,), (1,)), ((), ())), preferred_element_type=jnp.float32
    )


def pair_terms(
    query_heads,
    grad_heads,
    delta_rows,
    log_rows,
    query_docs,
    key_heads,
    value_heads,
    key_docs,
    score_scale,
):
    f32 = jnp.float32
    scores = (
        jnp.einsum("qhd,khd->hqk", query_heads, key_heads, preferred_element_type=f32) * score_scale
    )
    same = (query_docs[:, None] == key_docs[None, :])[None]
    probs = jnp.where(same, jnp.exp(scores - log_rows[:, :, None]), 0.0)
    grad_probs = jnp.einsum("qhd,khd->hqk", grad_heads, value_heads, preferred_element_type=f32)
    grad_scores_b = (probs * (grad_probs - jnp.transpose(delta_rows)[:, :, None])).astype(
        jnp.bfloat16
    )
    return (probs.astype(jnp.bfloat16), grad_scores_b)


def gram_of(iterate):
    highest = lax.Precision.HIGHEST
    owned_rows = iterate.shape[0] // lax.axis_size("ctx")
    picked = lax.slice_in_dim(iterate, 0, owned_rows * lax.axis_size("ctx"), axis=0)
    gram_share = lax.psum_scatter(
        jnp.dot(picked, iterate.T, precision=highest, preferred_element_type=jnp.float32).astype(
            jnp.bfloat16
        ),
        "ctx",
        scatter_dimension=0,
        tiled=True,
    ).astype(jnp.float32)
    return lax.all_gather(gram_share.astype(jnp.bfloat16), "ctx", axis=0, tiled=True).astype(
        gram_share.dtype
    )


def orthogonalize(moment):
    highest = lax.Precision.HIGHEST
    gram_matrix = gram_of(moment)
    inverse = 1.0 / (jnp.sqrt(jnp.trace(gram_matrix)) + ortho_eps)
    iterate = moment * inverse
    gram_matrix = gram_matrix * (inverse * inverse)
    for sweep_index in range(NS_ITERS):
        first_product = jnp.dot(gram_matrix, iterate, precision=highest)
        second_product = jnp.dot(gram_matrix, first_product, precision=highest)
        iterate = (
            quintic_one * iterate + quintic_two * first_product + quintic_three * second_product
        )
        if sweep_index + 1 < NS_ITERS:
            gram_matrix = gram_of(iterate)
    return iterate


def per_device(
    block_input,
    out_grad,
    positions,
    w_qkv,
    w_attn_out,
    w_in,
    w_mlp_out,
    norm_gains,
    m_qkv,
    m_attn_out,
    m_in,
    m_mlp_out,
    gain_mean,
    gain_var,
):
    bf16 = jnp.bfloat16
    f32 = jnp.float32
    dp_count = lax.axis_size("dp")
    ctx_count = lax.axis_size("ctx")
    tok_rows = block_input.shape[1]
    width = block_input.shape[2]
    heads = HEADS
    head_size = width // heads
    score_scale = 1.0 / math.sqrt(head_size)
    seq_length = tok_rows * ctx_count
    key_block = math.gcd(seq_length, 512)
    block_count = seq_length // key_block
    gathered = (
        lax.all_gather(w_qkv.astype(bf16), "dp", axis=0, tiled=True),
        lax.all_gather(w_attn_out.astype(bf16), "dp", axis=0, tiled=True),
        lax.all_gather(w_in.astype(bf16), "dp", axis=0, tiled=True),
        lax.all_gather(w_mlp_out.astype(bf16), "dp", axis=0, tiled=True),
        lax.all_gather(norm_gains.astype(bf16), "dp", axis=1, tiled=True),
    )
    w_qkv_b, w_out_b, w_in_b, w_mlp_b, gains_b = gathered
    gain_one = gains_b[0].astype(f32)
    gain_two = gains_b[1].astype(f32)
    x_wide = block_input[0].astype(f32)
    dy_seq = out_grad[0]
    hat_one, factor_one = normalize(x_wide)
    act_one = (hat_one * gain_one).astype(bf16)
    qkv = jnp.dot(act_one, w_qkv_b, preferred_element_type=f32)
    cosine, sine = rope_tables(positions[0], head_size)
    doc_own = (
        lax.axis_index("ctx") * tok_rows + jnp.arange(tok_rows, dtype=jnp.int32) - positions[0]
    )
    queries_b = rotate(qkv[:, :width].reshape(tok_rows, heads, head_size), cosine, sine).astype(
        bf16
    )
    keys_flat = (
        rotate(qkv[:, width : 2 * width].reshape(tok_rows, heads, head_size), cosine, sine)
        .astype(bf16)
        .reshape(tok_rows, width)
    )
    values_flat = qkv[:, 2 * width :].astype(bf16)
    key_piece = lax.all_gather(keys_flat, "ctx", axis=0, tiled=True)
    value_piece = lax.all_gather(values_flat, "ctx", axis=0, tiled=True)
    doc_piece = lax.all_gather(doc_own, "ctx", axis=0, tiled=True)
    rows_here = key_piece.shape[0]
    key_heads = key_piece.reshape(rows_here, heads, head_size)
    value_heads = value_piece.reshape(rows_here, heads, head_size)
    scores = (
        jnp.einsum("qhd,khd->hqk", queries_b, key_heads, preferred_element_type=f32) * score_scale
    )
    same = (doc_own[:, None] == doc_piece[None, :])[None]
    weights = jnp.where(same, jnp.exp(scores), 0.0)
    totals = jnp.sum(weights, axis=-1)
    summed = jnp.einsum(
        "hqk,khd->qhd", weights.astype(bf16), value_heads, preferred_element_type=f32
    )
    fold_result = (summed, totals)
    summed_values, total_weights = fold_result
    attended = summed_values / jnp.transpose(total_weights)[:, :, None]
    log_total = jnp.log(total_weights)
    mixed_b = attended.reshape(tok_rows, width).astype(bf16)
    hidden = x_wide + jnp.dot(mixed_b, w_out_b, preferred_element_type=f32)
    hat_two, factor_two = normalize(hidden)
    act_two = (hat_two * gain_two).astype(bf16)
    lifted = jnp.dot(act_two, w_in_b, preferred_element_type=f32)
    hidden_units = lifted.shape[1] // 2
    preact = lifted[:, :hidden_units]
    gate_half = lifted[:, hidden_units:]
    activated, derivative = gelu_parts(preact)
    inner_b = (activated * gate_half).astype(bf16)
    output = hidden + contract_cols(inner_b, w_mlp_b)
    dy_wide = dy_seq.astype(f32)
    grad_mlp = contract_rows(dy_seq, inner_b)
    grad_inner = jnp.dot(dy_seq, w_mlp_b, preferred_element_type=f32)
    grad_lift = jnp.concatenate(
        [grad_inner * gate_half * derivative, grad_inner * activated], axis=1
    ).astype(bf16)
    grad_in = contract_rows(act_two, grad_lift)
    grad_act_two = contract_cols(grad_lift, w_in_b)
    gain_grad_two = jnp.sum(grad_act_two * hat_two, axis=0)
    grad_hidden = dy_wide + normalize_back(grad_act_two * gain_two, hat_two, factor_two)
    grad_hidden_b = grad_hidden.astype(bf16)
    grad_out = contract_rows(mixed_b, grad_hidden_b)
    grad_mixed = contract_cols(grad_hidden_b, w_out_b).reshape(tok_rows, heads, head_size)
    delta = jnp.sum(grad_mixed * attended, axis=-1)
    grad_mixed_b = grad_mixed.astype(bf16)
    keys_all, values_all, docs_all = (
        lax.all_gather(keys_flat, "ctx", axis=0, tiled=True),
        lax.all_gather(values_flat, "ctx", axis=0, tiled=True),
        lax.all_gather(doc_own, "ctx", axis=0, tiled=True),
    )
    key_pieces = (
        keys_all.reshape(block_count, key_block, width),
        values_all.reshape(block_count, key_block, width),
        docs_all.reshape(block_count, key_block),
    )
    zero_query = jnp.zeros((tok_rows, heads, head_size), f32)

    def query_only_step(query_grad, pieces):
        key_piece, value_piece, doc_piece = pieces
        key_heads = key_piece.reshape(key_block, heads, head_size)
        value_heads = value_piece.reshape(key_block, heads, head_size)
        probs_b, grad_scores_b = pair_terms(
            queries_b,
            grad_mixed_b,
            delta,
            log_total,
            doc_own,
            key_heads,
            value_heads,
            doc_piece,
            score_scale,
        )
        query_grad = (
            query_grad
            + jnp.einsum("hqk,khd->qhd", grad_scores_b, key_heads, preferred_element_type=f32)
            * score_scale
        )
        return (query_grad, None)

    query_grad, unused_terms = lax.scan(query_only_step, zero_query, key_pieces)
    queries_all, grads_all, logs_all, deltas_all, qdocs_all = (
        lax.all_gather(queries_b.reshape(tok_rows, width), "ctx", axis=0, tiled=True),
        lax.all_gather(grad_mixed_b.reshape(tok_rows, width), "ctx", axis=0, tiled=True),
        lax.all_gather(log_total.astype(jnp.bfloat16), "ctx", axis=1, tiled=True).astype(
            log_total.dtype
        ),
        lax.all_gather(delta.astype(jnp.bfloat16), "ctx", axis=0, tiled=True).astype(delta.dtype),
        lax.all_gather(doc_own, "ctx", axis=0, tiled=True),
    )
    own_keys = keys_flat.reshape(tok_rows, heads, head_size)
    own_values = values_flat.reshape(tok_rows, heads, head_size)

    def key_side_step(carry, pieces):
        key_acc, value_acc = carry
        query_piece, grad_piece, log_piece, delta_piece, qdoc_piece = pieces
        query_heads = query_piece.reshape(key_block, heads, head_size)
        grad_heads = grad_piece.reshape(key_block, heads, head_size)
        probs_b, grad_scores_b = pair_terms(
            query_heads,
            grad_heads,
            delta_piece,
            log_piece,
            qdoc_piece,
            own_keys,
            own_values,
            doc_own,
            score_scale,
        )
        value_acc = value_acc + jnp.einsum(
            "hqk,qhd->khd", probs_b, grad_heads, preferred_element_type=f32
        )
        key_acc = (
            key_acc
            + jnp.einsum("hqk,qhd->khd", grad_scores_b, query_heads, preferred_element_type=f32)
            * score_scale
        )
        return ((key_acc, value_acc), None)

    query_pieces = (
        queries_all.reshape(block_count, key_block, width),
        grads_all.reshape(block_count, key_block, width),
        jnp.transpose(logs_all.reshape(heads, block_count, key_block), (1, 0, 2)),
        deltas_all.reshape(block_count, key_block, heads),
        qdocs_all.reshape(block_count, key_block),
    )
    (key_acc, value_acc), unused_side = lax.scan(
        key_side_step, (zero_query, zero_query), query_pieces
    )
    key_grad = key_acc.reshape(tok_rows, width)
    value_grad = value_acc.reshape(tok_rows, width)
    grad_qkv_in = jnp.concatenate(
        [
            rotate_back(query_grad, cosine, sine).reshape(tok_rows, width),
            rotate_back(key_grad.reshape(tok_rows, heads, head_size), cosine, sine).reshape(
                tok_rows, width
            ),
            value_grad,
        ],
        axis=1,
    ).astype(bf16)
    grad_qkv = contract_rows(act_one, grad_qkv_in)
    grad_act_one = contract_cols(grad_qkv_in, w_qkv_b)
    gain_grad_one = jnp.sum(grad_act_one * hat_one, axis=0)
    grad_input = grad_hidden + normalize_back(grad_act_one * gain_one, hat_one, factor_one)
    gain_grads = jnp.stack([gain_grad_one, gain_grad_two])
    shares = (
        lax.psum_scatter(
            grad_qkv.astype(jnp.bfloat16), "dp", scatter_dimension=0, tiled=True
        ).astype(jnp.float32),
        lax.psum_scatter(
            grad_out.astype(jnp.bfloat16), "dp", scatter_dimension=0, tiled=True
        ).astype(jnp.float32),
        lax.psum_scatter(
            grad_in.astype(jnp.bfloat16), "dp", scatter_dimension=0, tiled=True
        ).astype(jnp.float32),
        lax.psum_scatter(
            grad_mlp.astype(jnp.bfloat16), "dp", scatter_dimension=0, tiled=True
        ).astype(jnp.float32),
        lax.psum_scatter(
            gain_grads.astype(jnp.bfloat16), "dp", scatter_dimension=1, tiled=True
        ).astype(jnp.float32),
    )
    summed_grads = (
        lax.psum(shares[0].astype(jnp.bfloat16), "ctx").astype(jnp.float32),
        lax.psum(shares[1].astype(jnp.bfloat16), "ctx").astype(jnp.float32),
        lax.psum(shares[2].astype(jnp.bfloat16), "ctx").astype(jnp.float32),
        lax.psum(shares[3].astype(jnp.bfloat16), "ctx").astype(jnp.float32),
        lax.psum(shares[4].astype(jnp.bfloat16), "ctx").astype(jnp.float32),
    )
    factor = 1.0 / math.sqrt(dp_count * ctx_count * tok_rows)
    grads = [total * factor for total in summed_grads]
    matrices = (w_qkv, w_attn_out, w_in, w_mlp_out)
    moments = (m_qkv, m_attn_out, m_in, m_mlp_out)
    moments_next = [momentum_rate * moment + grad for moment, grad in zip(moments, grads[:4])]
    owned_rows = w_qkv.shape[0]
    widest = max(w_qkv.shape[1], w_in.shape[1])
    col_count = widest // ctx_count
    ctx_place = lax.axis_index("ctx")

    def owner_slice(matrix):
        padded = jnp.pad(matrix, ((0, 0), (0, widest - matrix.shape[1])))
        return lax.dynamic_slice_in_dim(padded, ctx_place * col_count, col_count, 1)

    filled_slots = jnp.stack([owner_slice(moment) for moment in moments_next])
    empty_slots = jnp.zeros((dp_count - 4, owned_rows, col_count), f32)
    send_buffer = jnp.concatenate([filled_slots, empty_slots], axis=0)
    received = lax.all_to_all(
        send_buffer.astype(jnp.bfloat16), "dp", split_axis=0, concat_axis=0, tiled=True
    ).astype(send_buffer.dtype)
    owned_matrix = received.reshape(dp_count * owned_rows, col_count)
    orthogonal = orthogonalize(owned_matrix)
    returned = lax.all_to_all(
        shortened(orthogonal.reshape(dp_count, owned_rows, col_count)),
        "dp",
        split_axis=0,
        concat_axis=0,
        tiled=True,
    )
    updates = lax.all_gather(shortened(returned[:4]), "ctx", axis=2, tiled=True)
    new_weights = []
    for slot_index in range(4):
        weight = matrices[slot_index]
        full_rows = weight.shape[0] * dp_count
        rate = matrix_rate * math.sqrt(max(full_rows, weight.shape[1]))
        new_weights.append(weight - rate * updates[slot_index][:, : weight.shape[1]])
    gain_grad = grads[4]
    mean_next = beta_first * gain_mean + (1.0 - beta_first) * gain_grad
    var_next = beta_second * gain_var + (1.0 - beta_second) * gain_grad * gain_grad
    gains_next = norm_gains - gain_rate * (mean_next / first_fix) / (
        jnp.sqrt(var_next / second_fix) + adam_eps
    )
    return (
        output.astype(bf16)[None],
        grad_input[None],
        grads[0],
        grads[1],
        grads[2],
        grads[3],
        gain_grad,
        new_weights[0],
        new_weights[1],
        new_weights[2],
        new_weights[3],
        gains_next,
        moments_next[0],
        moments_next[1],
        moments_next[2],
        moments_next[3],
        mean_next,
        var_next,
    )


def ring_places(mesh):
    chip_count = mesh.shape["dp"] // 2
    natural = list(range(chip_count))
    try:
        column = [mesh.devices[2 * chip, 0] for chip in natural]
        partner = [mesh.devices[2 * chip + 1, 0] for chip in natural]
        coords = [tuple(device.coords) for device in column]
        if coords != [tuple(device.coords) for device in partner]:
            return natural
    except (AttributeError, IndexError):
        return natural
    dims = [dim for dim in range(3) if len({c[dim] for c in coords}) > 1]
    narrow = [dim for dim in dims if len({c[dim] for c in coords}) == 2]
    if len(dims) != 2 or not narrow:
        return natural
    split = narrow[0]
    along = [dim for dim in dims if dim != split][0]
    low = min(c[split] for c in coords)
    first = sorted((c for c in natural if coords[c][split] == low), key=lambda c: coords[c][along])
    second = sorted((c for c in natural if coords[c][split] != low), key=lambda c: -coords[c][along])
    return first + second


def dot_nn(left, right):
    return lax.dot_general(
        left, right, (((1,), (0,)), ((), ())), preferred_element_type=jnp.float32
    )


def lane_iota(shape):
    return lax.broadcasted_iota(jnp.int32, shape, len(shape) - 1)


def turn_lanes(field, head_size):
    size = field.shape[-1]
    half = head_size // 2
    up = pltpu.roll(field, size - half, field.ndim - 1)
    down = pltpu.roll(field, half, field.ndim - 1)
    return jnp.where(lane_iota(field.shape) % head_size < half, up, down)


def repeat_lanes(table, count):
    return jnp.concatenate([table] * count, axis=1)


def whole_spec():
    return pl.BlockSpec(memory_space=pltpu.VMEM)


def run_whole(body, index_row, inputs, outputs, scratch=()):
    return pl.pallas_call(
        body,
        in_specs=[pl.BlockSpec(memory_space=pltpu.SMEM)] + [whole_spec()] * len(inputs),
        out_specs=[whole_spec()] * len(outputs),
        out_shape=[jax.ShapeDtypeStruct(shape, dtype) for shape, dtype in outputs],
        scratch_shapes=list(scratch),
        compiler_params=pltpu.CompilerParams(vmem_limit_bytes=56 * 1024 * 1024),
    )(index_row, *inputs)


def attend_stage(plan, index_row, own_pack, other_pack, cosine, sine, starts, pieces):
    bf16, f32 = jnp.bfloat16, jnp.float32
    tok, length, width, span, head_size = plan
    count = len(pieces)
    rows = pieces[0].shape[0]
    score_scale = 1.0 / math.sqrt(head_size)
    start_col = starts[:, None]
    start_row = starts[None, :]

    def body(index_ref, own_ref, other_ref, cos_ref, sin_ref, col_ref, row_ref, *rest):
        piece_refs = rest[:count]
        x_ref, dy_ref, a_ref, q_ref, k_ref, v_ref, o_ref, ob_ref, lse_ref, g_ref, w_ref = rest[
            count : count + 11
        ]
        gain_ref = rest[-1]
        half_at = index_ref[count]
        own_at = pl.multiple_of(half_at * tok, tok)
        other_at = pl.multiple_of((1 - half_at) * tok, tok)
        x_ref[pl.ds(own_at, tok), :] = own_ref[:tok, :]
        x_ref[pl.ds(other_at, tok), :] = other_ref[:tok, :]
        dy_ref[pl.ds(own_at, tok), :] = own_ref[tok : 2 * tok, :]
        dy_ref[pl.ds(other_at, tok), :] = other_ref[tok : 2 * tok, :]
        for piece_at in range(count):
            at = pl.ds(pl.multiple_of(index_ref[piece_at] * rows, rows), rows)
            w_ref[at, :] = piece_refs[piece_at][:, : 3 * span]
            gain_ref[at, :] = piece_refs[piece_at][:, 3 * span :].astype(f32)
        gain_rows = jnp.transpose(gain_ref[...])
        g_ref[...] = gain_rows[:8]
        hat, _ = normalize(x_ref[...].astype(f32))
        act = (hat * gain_rows[:1]).astype(bf16)
        a_ref[...] = act
        cos_wide = repeat_lanes(cos_ref[...], span // 128)
        sin_wide = repeat_lanes(sin_ref[...], span // 128)
        queries = dot_nn(act, w_ref[:, :span])
        q_ref[...] = (queries * cos_wide + turn_lanes(queries, head_size) * sin_wide).astype(bf16)
        keys = dot_nn(act, w_ref[:, span : 2 * span])
        k_ref[...] = (keys * cos_wide + turn_lanes(keys, head_size) * sin_wide).astype(bf16)
        v_ref[...] = dot_nn(act, w_ref[:, 2 * span :]).astype(bf16)
        same = col_ref[...] == row_ref[...]
        low = lane_iota((length, 128)) < head_size
        lanes = lane_iota((length, 128))
        logs = jnp.zeros((length, 128), f32)
        for pair in range(span // 128):
            cols = slice(pair * 128, pair * 128 + 128)
            query, key, value = q_ref[:, cols], k_ref[:, cols], v_ref[:, cols]
            parts = []
            for side in range(2):
                mine = low if side == 0 else jnp.logical_not(low)
                score = contract_cols(jnp.where(mine, query, 0), key) * score_scale
                weight = jnp.where(same, jnp.exp(score), 0.0)
                total = jnp.sum(weight, axis=1, keepdims=True)
                parts.append(dot_nn(weight.astype(bf16), value) / total)
                logs = jnp.where(lanes == 2 * pair + side, jnp.log(total), logs)
            mixed = jnp.where(low, parts[0], parts[1])
            o_ref[:, cols] = mixed
            ob_ref[:, cols] = mixed.astype(bf16)
        lse_ref[...] = logs

    return run_whole(
        body,
        index_row,
        [own_pack, other_pack, cosine, sine, start_col, start_row, *pieces],
        [
            ((length, width), bf16),
            ((length, width), bf16),
            ((length, width), bf16),
            ((length, span), bf16),
            ((length, span), bf16),
            ((length, span), bf16),
            ((length, span), f32),
            ((length, span), bf16),
            ((length, 128), f32),
            ((8, width), f32),
            ((width, 3 * span), bf16),
        ],
        [pltpu.VMEM((width, 128), f32)],
    )


def lift_stage(plan, index_row, x, dy, own_mixed, other_mixed, gains, pieces):
    bf16, f32 = jnp.bfloat16, jnp.float32
    tok, length, width, span, units, core_units = plan
    count = len(pieces)
    rows = pieces[0].shape[0]
    rest_units = units - core_units

    def body(index_ref, x_ref, dy_ref, own_ref, other_ref, g_ref, *rest):
        piece_refs = rest[:count]
        (
            wo_ref,
            wm_ref,
            h_ref,
            hat_ref,
            r_ref,
            a_ref,
            z_ref,
            dp_ref,
            dg_ref,
            part_ref,
            send_ref,
        ) = rest[count : count + 11]
        wp_ref, wg_ref = rest[-2:]
        half_at = index_ref[count]
        low = lane_iota((rows, 128)) < rest_units
        zero = jnp.zeros((rows, 128), bf16)
        edge = width + 3 * core_units
        for piece_at in range(count):
            at = pl.ds(pl.multiple_of(index_ref[piece_at] * rows, rows), rows)
            piece = piece_refs[piece_at]
            wo_ref[at, :] = piece[:, :width]
            wp_ref[at, :core_units] = piece[:, width : width + core_units]
            wg_ref[at, :core_units] = piece[:, width + core_units : width + 2 * core_units]
            wm_ref[at, :core_units] = piece[:, width + 2 * core_units : edge]
            both = piece[:, edge : edge + 128]
            wp_ref[at, core_units:] = jnp.where(low, both, zero)
            turned = pltpu.roll(both.astype(f32), 128 - rest_units, 1).astype(bf16)
            wg_ref[at, core_units:] = jnp.where(low, turned, zero)
            wm_ref[at, core_units:] = piece[:, edge + 128 : edge + 256]
        own_at = pl.multiple_of(half_at * span, span)
        other_at = pl.multiple_of((1 - half_at) * span, span)
        hidden = (
            x_ref[...].astype(f32)
            + dot_nn(own_ref[...], wo_ref[pl.ds(own_at, span), :])
            + dot_nn(other_ref[...], wo_ref[pl.ds(other_at, span), :])
        )
        h_ref[...] = hidden
        hat, factor = normalize(hidden)
        hat_ref[...] = hat
        r_ref[...] = jnp.broadcast_to(factor, r_ref.shape)
        act = (hat * g_ref[1:2, :]).astype(bf16)
        a_ref[...] = act
        preact = dot_nn(act, wp_ref[...])
        gate = dot_nn(act, wg_ref[...])
        activated, derivative = gelu_parts(preact)
        z_ref[...] = (activated * gate).astype(bf16)
        grad_inner = dot_nn(dy_ref[...], wm_ref[...])
        grad_pre = (grad_inner * gate * derivative).astype(bf16)
        grad_gate = (grad_inner * activated).astype(bf16)
        dp_ref[...] = grad_pre
        dg_ref[...] = grad_gate
        part = contract_cols(grad_pre, wp_ref[...]) + contract_cols(grad_gate, wg_ref[...])
        part_ref[...] = part
        send_ref[...] = part.astype(bf16)

    wide = core_units + 128
    return run_whole(
        body,
        index_row,
        [x, dy, own_mixed, other_mixed, gains, *pieces],
        [
            ((width, width), bf16),
            ((width, wide), bf16),
            ((length, width), f32),
            ((length, width), f32),
            ((length, 128), f32),
            ((length, width), bf16),
            ((length, wide), bf16),
            ((length, wide), bf16),
            ((length, wide), bf16),
            ((length, width), f32),
            ((length, width), bf16),
        ],
        [pltpu.VMEM((width, wide), bf16), pltpu.VMEM((width, wide), bf16)],
    )


def deal_rows(index_ref, base, core_at, rows, chips, scratch_ref, kept_ref, given_ref):
    for step in range(chips):
        chip = index_ref[base + step]
        kept_at = pl.multiple_of((2 * chip + core_at) * rows, rows)
        given_at = pl.multiple_of((2 * chip + 1 - core_at) * rows, rows)
        kept_ref[step] = scratch_ref[pl.ds(kept_at, rows), :].astype(kept_ref.dtype)
        given_ref[step] = scratch_ref[pl.ds(given_at, rows), :].astype(given_ref.dtype)


def early_stage(plan, index_row, dy, act, inner, grad_pre, grad_gate, w_mlp, hidden, part, hat):
    bf16, f32 = jnp.bfloat16, jnp.float32
    tok, length, width, units, core_units, chips, rows = plan
    rest_units = units - core_units
    columns = 3 * core_units + 256
    count = 2 * chips

    def body(index_ref, dy_ref, a_ref, z_ref, dp_ref, dg_ref, wm_ref, h_ref, part_ref, hat_ref, *rest):
        kept_ref, given_ref, out_ref, send_ref, gg_ref, whole_ref = rest
        half_at = index_ref[count]
        core_at = index_ref[count + 1]
        grad_pre_w = contract_rows(a_ref[...], dp_ref[...])
        whole_ref[:, :core_units] = grad_pre_w[:, :core_units]
        grad_gate_w = contract_rows(a_ref[...], dg_ref[...])
        whole_ref[:, core_units : 2 * core_units] = grad_gate_w[:, :core_units]
        low = lane_iota((width, 128)) < rest_units
        turned = pltpu.roll(grad_gate_w[:, core_units:], rest_units, 1)
        whole_ref[:, 3 * core_units : 3 * core_units + 128] = jnp.where(
            low, grad_pre_w[:, core_units:], turned
        )
        grad_mlp = contract_rows(dy_ref[...], z_ref[...])
        whole_ref[:, 2 * core_units : 3 * core_units] = grad_mlp[:, :core_units]
        whole_ref[:, 3 * core_units + 128 :] = grad_mlp[:, core_units:]
        deal_rows(index_ref, count + 2, core_at, rows, chips, whole_ref, kept_ref, given_ref)
        own_at = pl.multiple_of(half_at * tok, tok)
        other_at = pl.multiple_of((1 - half_at) * tok, tok)
        out_ref[...] = h_ref[pl.ds(own_at, tok), :] + contract_cols(
            z_ref[pl.ds(own_at, tok), :], wm_ref[...]
        )
        send_ref[...] = contract_cols(z_ref[pl.ds(other_at, tok), :], wm_ref[...]).astype(bf16)
        gg = jnp.sum(part_ref[...] * hat_ref[...], axis=0, keepdims=True)
        gg_ref[...] = jnp.broadcast_to(gg, gg_ref.shape)

    return run_whole(
        body,
        index_row,
        [dy, act, inner, grad_pre, grad_gate, w_mlp, hidden, part, hat],
        [
            ((chips, rows, columns), bf16),
            ((chips, rows, columns), bf16),
            ((tok, width), f32),
            ((tok, width), bf16),
            ((8, width), f32),
        ],
        [pltpu.VMEM((width, columns), f32)],
    )


def late_stage(plan, index_row, inputs):
    bf16, f32 = jnp.bfloat16, jnp.float32
    tok, length, width, span, head_size, chips, rows = plan
    score_scale = 1.0 / math.sqrt(head_size)
    columns = 4 * span + 128
    count = 2 * chips

    def body(index_ref, *refs):
        (
            part_ref,
            other_part_ref,
            hat_ref,
            r_ref,
            dy_ref,
            g_ref,
            gg_ref,
            wo_ref,
            wq_ref,
            x_ref,
            a_ref,
            q_ref,
            k_ref,
            v_ref,
            o_ref,
            lse_ref,
            cos_ref,
            sin_ref,
            col_ref,
            row_ref,
            own_ref,
            other_ref,
            kept_ref,
            given_ref,
            dh_ref,
            da_ref,
            send_ref,
            whole_ref,
            do_ref,
            dqkv_ref,
        ) = refs
        half_at = index_ref[count]
        core_at = index_ref[count + 1]
        gain_one = g_ref[0:1, :]
        gain_two = g_ref[1:2, :]
        grad_act = part_ref[...] + other_part_ref[...].astype(f32)
        grad_hidden = dy_ref[...].astype(f32) + normalize_back(
            grad_act * gain_two, hat_ref[...], r_ref[:, 0:1]
        )
        grad_b = grad_hidden.astype(bf16)
        own_span = pl.multiple_of(half_at * span, span)
        other_span = pl.multiple_of((1 - half_at) * span, span)
        own_tok = pl.multiple_of(half_at * tok, tok)
        other_tok = pl.multiple_of((1 - half_at) * tok, tok)
        do_ref[...] = contract_cols(grad_b, wo_ref[pl.ds(own_span, span), :])
        same = col_ref[...] == row_ref[...]
        low = lane_iota((length, 128)) < head_size
        cos, sin = cos_ref[...], sin_ref[...]
        for pair in range(span // 128):
            cols = slice(pair * 128, pair * 128 + 128)
            query, key, value = q_ref[:, cols], k_ref[:, cols], v_ref[:, cols]
            grad_o = do_ref[:, cols]
            grad_ob = grad_o.astype(bf16)
            product = grad_o * o_ref[:, cols]
            found = []
            for side in range(2):
                head = 2 * pair + side
                mine = low if side == 0 else jnp.logical_not(low)
                delta = jnp.sum(jnp.where(mine, product, 0.0), axis=1, keepdims=True)
                score = contract_cols(jnp.where(mine, query, 0), key) * score_scale
                probs = jnp.where(same, jnp.exp(score - lse_ref[:, head : head + 1]), 0.0)
                grad_probs = contract_cols(jnp.where(mine, grad_ob, 0), value)
                grad_score = (probs * (grad_probs - delta)).astype(bf16)
                found.append(
                    (
                        dot_nn(grad_score, key) * score_scale,
                        contract_rows(grad_score, query) * score_scale,
                        contract_rows(probs.astype(bf16), grad_ob),
                    )
                )
            grad_q, grad_k, grad_v = (
                jnp.where(low, even, odd) for even, odd in zip(found[0], found[1])
            )
            base = pair * 128
            dqkv_ref[:, base : base + 128] = (
                grad_q * cos - turn_lanes(grad_q, head_size) * sin
            ).astype(bf16)
            dqkv_ref[:, span + base : span + base + 128] = (
                grad_k * cos - turn_lanes(grad_k, head_size) * sin
            ).astype(bf16)
            dqkv_ref[:, 2 * span + base : 2 * span + base + 128] = grad_v.astype(bf16)
        whole_ref[:, : 3 * span] = contract_rows(a_ref[...], dqkv_ref[...])
        half_b = jnp.where(half_at == 0, grad_hidden[:, :span], grad_hidden[:, span:]).astype(bf16)
        whole_ref[pl.ds(own_span, span), 3 * span : 4 * span] = contract_rows(own_ref[...], half_b)
        whole_ref[pl.ds(other_span, span), 3 * span : 4 * span] = contract_rows(
            other_ref[...], half_b
        )
        grad_one = contract_cols(dqkv_ref[...], wq_ref[...])
        hat_one, _ = normalize(x_ref[...].astype(f32))
        gg_one = jnp.sum(grad_one * hat_one, axis=0, keepdims=True)
        row_at = lax.broadcasted_iota(jnp.int32, (128, width), 0)
        gain_rows = jnp.where(row_at == 0, gg_one, jnp.where(row_at == 1, gg_ref[0:1, :], 0.0))
        whole_ref[:, 4 * span :] = jnp.transpose(gain_rows)
        deal_rows(index_ref, count + 2, core_at, rows, chips, whole_ref, kept_ref, given_ref)
        part_own = part_ref[pl.ds(own_tok, tok), :] + other_part_ref[pl.ds(own_tok, tok), :].astype(
            f32
        )
        dh_ref[...] = dy_ref[pl.ds(own_tok, tok), :].astype(f32) + normalize_back(
            part_own * gain_two, hat_ref[pl.ds(own_tok, tok), :], r_ref[pl.ds(own_tok, tok), 0:1]
        )
        da_ref[...] = contract_cols(dqkv_ref[pl.ds(own_tok, tok), :], wq_ref[...])
        send_ref[...] = contract_cols(dqkv_ref[pl.ds(other_tok, tok), :], wq_ref[...]).astype(bf16)

    return run_whole(
        body,
        index_row,
        inputs,
        [
            ((chips, rows, columns), bf16),
            ((chips, rows, columns), bf16),
            ((tok, width), f32),
            ((tok, width), f32),
            ((tok, width), bf16),
        ],
        [
            pltpu.VMEM((width, columns), f32),
            pltpu.VMEM((length, span), f32),
            pltpu.VMEM((length, 3 * span), bf16),
        ],
    )


def sweep_rows(start_rows, picked_rows):
    high = lax.Precision.HIGH
    f32 = jnp.float32
    gram = contract_cols(start_rows, start_rows)
    inverse = 1.0 / (jnp.sqrt(jnp.trace(gram)) + ortho_eps)
    gram = gram * (inverse * inverse)
    identity = jnp.eye(gram.shape[0], dtype=f32)
    top = None
    for sweep_index in range(NS_ITERS):
        last = sweep_index + 1 == NS_ITERS
        if last and top is not None:
            inner = quintic_two * top + quintic_three * jnp.dot(top, gram, precision=high)
            top = quintic_one * top + jnp.dot(inner, gram, precision=high)
            break
        square = jnp.dot(gram, gram, precision=high)
        factor = quintic_one * identity + quintic_two * gram + quintic_three * square
        if top is None:
            top = factor[:picked_rows]
        else:
            top = jnp.dot(top, factor, precision=high)
        if not last:
            gram = jnp.dot(jnp.dot(gram, factor, precision=high), factor, precision=high)
    return jnp.dot((top * inverse).astype(jnp.bfloat16), start_rows, preferred_element_type=f32)


def paired_device(order, *arrays):
    (
        block_input,
        out_grad,
        positions,
        w_qkv,
        w_attn_out,
        w_in,
        w_mlp_out,
        norm_gains,
        m_qkv,
        m_attn_out,
        m_in,
        m_mlp_out,
        gain_mean,
        gain_var,
    ) = arrays
    bf16 = jnp.bfloat16
    f32 = jnp.float32
    dp_count = lax.axis_size("dp")
    ctx_count = lax.axis_size("ctx")
    chip_count = dp_count // 2
    dp_at = lax.axis_index("dp")
    half_at = lax.axis_index("ctx")
    low_half = half_at == 0
    core_at = dp_at % 2
    tok_rows = block_input.shape[1]
    width = block_input.shape[2]
    length = tok_rows * ctx_count
    heads = HEADS // ctx_count
    head_size = width // HEADS
    span = heads * head_size
    score_scale = 1.0 / math.sqrt(head_size)
    owned_rows = w_qkv.shape[0]
    hidden_units = w_mlp_out.shape[1]
    hidden_half = hidden_units // 2
    place = [0] * chip_count
    for spot, chip in enumerate(order):
        place[chip] = spot

    def ring_pairs(step):
        return [
            (2 * order[spot] + core, 2 * order[(spot + step) % chip_count] + core)
            for spot in range(chip_count)
            for core in range(2)
        ]

    forward_pairs = ring_pairs(1)
    backward_pairs = ring_pairs(-1)
    core_pairs = [(index, index ^ 1) for index in range(dp_count)]
    flip_pairs = [(0, 1), (1, 0)]

    def swap_core(value):
        return lax.ppermute(value, "dp", core_pairs)

    def swap_half(value):
        return lax.ppermute(value, "ctx", flip_pairs)

    ahead_steps = chip_count // 2
    behind_steps = chip_count - 1 - ahead_steps

    piece_steps = [0]
    for step in range(1, ahead_steps + 1):
        piece_steps.append(-step)
        if step <= behind_steps:
            piece_steps.append(step)

    index_rows = []
    for index in range(dp_count):
        spot, core = place[index // 2], index % 2
        chips_at = [order[(spot + step) % chip_count] for step in piece_steps]
        ring_at = [order[(spot + step) % chip_count] for step in range(chip_count)]
        for half in range(ctx_count):
            row = [2 * chip + core for chip in chips_at] + [2 * chip + 1 - core for chip in chips_at]
            index_rows.append(row + [half, core] + ring_at)
    index_row = lax.dynamic_index_in_dim(
        jnp.array(index_rows, jnp.int32), dp_at * ctx_count + half_at, 0, keepdims=False
    )

    def ring_collect(shard):
        pieces = [shard]
        ahead = shard
        behind = shard
        for step in range(1, ahead_steps + 1):
            ahead = lax.ppermute(ahead, "dp", forward_pairs)
            pieces.append(ahead)
            if step <= behind_steps:
                behind = lax.ppermute(behind, "dp", backward_pairs)
                pieces.append(behind)
        return pieces

    def collect(shard):
        pieces = ring_collect(shard)
        return pieces + [swap_core(piece) for piece in pieces]

    def ring_reduce(kept, given):
        chunks = (kept.astype(f32) + swap_core(given).astype(f32)).astype(bf16)
        ahead = chunks[ahead_steps]
        behind = chunks[chip_count - behind_steps]
        for step in range(ahead_steps, 0, -1):
            ahead = lax.ppermute(ahead, "dp", forward_pairs)
            if step > 1:
                ahead = (ahead.astype(f32) + chunks[step - 1].astype(f32)).astype(bf16)
            if step <= behind_steps:
                behind = lax.ppermute(behind, "dp", backward_pairs)
                if step > 1:
                    nearer = chunks[chip_count + 1 - step]
                    behind = (behind.astype(f32) + nearer.astype(f32)).astype(bf16)
        return (chunks[0].astype(f32) + ahead.astype(f32) + behind.astype(f32)).astype(bf16)

    def my_half(matrix, parts):
        rows = matrix.shape[0]
        split = matrix.reshape(rows, parts, 2, -1)
        picked = jnp.where(low_half, split[:, :, 0], split[:, :, 1])
        return picked.reshape(rows, -1)

    def ordered(own, other, axis):
        first = jnp.where(low_half, own, other)
        second = jnp.where(low_half, other, own)
        return jnp.concatenate([first, second], axis=axis)

    gain_columns = jnp.pad(jnp.transpose(norm_gains), ((0, 0), (0, 128 - norm_gains.shape[0])))
    first_shard = jnp.concatenate([my_half(w_qkv, 3), gain_columns], axis=1).astype(bf16)
    core_units = hidden_half // 128 * 128
    rest_units = hidden_half - core_units
    lift_h = my_half(w_in, 2)
    lift_p, lift_g = lift_h[:, :hidden_half], lift_h[:, hidden_half:]
    drop_h = my_half(w_mlp_out, 1)
    second_shard = jnp.concatenate(
        [
            w_attn_out,
            lift_p[:, :core_units],
            lift_g[:, :core_units],
            drop_h[:, :core_units],
            lift_p[:, core_units:],
            lift_g[:, core_units:],
            drop_h[:, core_units:],
            jnp.zeros((owned_rows, 128 - rest_units), f32),
        ],
        axis=1,
    ).astype(bf16)

    own_places = positions[0]
    digits = jnp.stack([own_places // 128, own_places % 128]).astype(bf16)
    digit_rows = jnp.pad(digits, ((0, 14), (0, width - tok_rows)))
    own_pack = jnp.concatenate([block_input[0], out_grad[0], digit_rows], axis=0)
    other_pack = swap_half(own_pack)
    first_pieces = collect(first_shard)
    second_pieces = collect(second_shard)

    other_digits = other_pack[2 * tok_rows : 2 * tok_rows + 2, :tok_rows].astype(jnp.int32)
    places = ordered(own_places, other_digits[0] * 128 + other_digits[1], 0)
    lanes = jnp.arange(128, dtype=jnp.int32)
    indices = (lanes % (head_size // 2)).astype(f32)
    frequency = jnp.exp(indices * (-2.0 * math.log(theta_base) / head_size))
    angles = places.astype(f32)[:, None] * frequency[None, :]
    cosine = jnp.cos(angles)
    sine = jnp.where((lanes % head_size < head_size // 2)[None, :], -1.0, 1.0) * jnp.sin(angles)
    starts = jnp.arange(length, dtype=jnp.int32) - places

    x, dy, act_one, queries, keys, values, mixed, own_mixed, logs, gains, w_qkv_h = attend_stage(
        (tok_rows, length, width, span, head_size),
        index_row,
        own_pack,
        other_pack,
        cosine,
        sine,
        starts,
        first_pieces,
    )
    other_mixed = swap_half(own_mixed)
    (
        w_out_b,
        w_mlp_h,
        hidden,
        hat_two,
        factor_two,
        act_two,
        inner,
        grad_pre,
        grad_gate,
        grad_two_part,
        grad_two_send,
    ) = lift_stage(
        (tok_rows, length, width, span, hidden_half, core_units),
        index_row,
        x,
        dy,
        own_mixed,
        other_mixed,
        gains,
        second_pieces,
    )
    other_two_part = swap_half(grad_two_send)
    early_kept, early_given, out_own, out_send, gain_two_grad = early_stage(
        (tok_rows, length, width, hidden_half, core_units, chip_count, owned_rows),
        index_row,
        dy,
        act_two,
        inner,
        grad_pre,
        grad_gate,
        w_mlp_h,
        hidden,
        grad_two_part,
        hat_two,
    )
    early_rows = ring_reduce(early_kept, early_given)
    output = out_own + swap_half(out_send).astype(f32)
    late_kept, late_given, grad_hidden_own, grad_one_own, grad_one_send = late_stage(
        (tok_rows, length, width, span, head_size, chip_count, owned_rows),
        index_row,
        [
            grad_two_part,
            other_two_part,
            hat_two,
            factor_two,
            dy,
            gains,
            gain_two_grad,
            w_out_b,
            w_qkv_h,
            x,
            act_one,
            queries,
            keys,
            values,
            mixed,
            logs,
            cosine,
            sine,
            starts[:, None],
            starts[None, :],
            own_mixed,
            other_mixed,
        ],
    )
    late_rows = ring_reduce(late_kept, late_given)
    grad_act_one = grad_one_own + swap_half(grad_one_send).astype(f32)
    hat_own, factor_own = normalize(block_input[0].astype(f32))
    grad_input = grad_hidden_own + normalize_back(grad_act_one * gains[0], hat_own, factor_own)

    def whole_columns(own, other, parts):
        rows = own.shape[0]
        first = jnp.where(low_half, own, other).reshape(rows, parts, -1)
        second = jnp.where(low_half, other, own).reshape(rows, parts, -1)
        return jnp.stack([first, second], axis=2).reshape(rows, -1).astype(f32)

    factor = 1.0 / math.sqrt(dp_count * length)
    late_other = swap_half(late_rows)

    def unpacked(rows):
        edge = 3 * core_units
        return jnp.concatenate(
            [
                rows[:, :core_units],
                rows[:, edge : edge + rest_units],
                rows[:, core_units : 2 * core_units],
                rows[:, edge + rest_units : edge + 2 * rest_units],
                rows[:, 2 * core_units : edge],
                rows[:, edge + 128 : edge + 128 + rest_units],
            ],
            axis=1,
        )

    early_other = unpacked(swap_half(early_rows))
    early_rows = unpacked(early_rows)
    cut = 2 * hidden_half
    grads = [
        whole_columns(late_rows[:, : 3 * span], late_other[:, : 3 * span], 3) * factor,
        whole_columns(
            late_rows[:, 3 * span : 3 * span + span], late_other[:, 3 * span : 3 * span + span], 1
        )
        * factor,
        whole_columns(early_rows[:, :cut], early_other[:, :cut], 2) * factor,
        whole_columns(early_rows[:, cut:], early_other[:, cut:], 1) * factor,
    ]
    gain_sum = late_rows[:, 4 * span :].astype(f32) + late_other[:, 4 * span :].astype(f32)
    gain_grad = jnp.transpose(gain_sum)[:2] * factor

    matrices = (w_qkv, w_attn_out, w_in, w_mlp_out)
    moments = (m_qkv, m_attn_out, m_in, m_mlp_out)
    moments_next = [momentum_rate * moment + grad for moment, grad in zip(moments, grads)]
    widest = max(moment.shape[1] for moment in moments)
    slots = jnp.stack(
        [
            jnp.pad(moment.astype(bf16), ((0, 0), (0, widest - moment.shape[1])))
            for moment in moments_next
        ]
    )
    group = dp_count // 4
    group_at = dp_at // group

    def shift_pairs(step):
        return [(index, (index + step * group) % dp_count) for index in range(dp_count)]

    blocks = [lax.dynamic_index_in_dim(slots, group_at, 0, keepdims=False)]
    for step in range(1, 4):
        given = lax.dynamic_index_in_dim(slots, (group_at + step) % 4, 0, keepdims=False)
        blocks.append(lax.ppermute(given, "dp", shift_pairs(step)))
    held = jnp.concatenate(blocks, axis=0)
    reach = 2
    while reach < group:
        pairs = [(index, index ^ reach) for index in range(dp_count)]
        held = jnp.concatenate([held, lax.ppermute(held, "dp", pairs)], axis=0)
        reach *= 2
    held = jnp.concatenate([held, swap_core(held)], axis=0)
    turned = sweep_rows(held, 4 * owned_rows).astype(bf16).reshape(4, owned_rows, widest)
    returned = [turned[0]]
    for step in range(1, 4):
        returned.append(lax.ppermute(turned[step], "dp", shift_pairs(-step)))
    updates = jnp.stack(returned)
    new_weights = []
    for slot_index, weight in enumerate(matrices):
        update = lax.dynamic_index_in_dim(updates, (slot_index - group_at + 4) % 4, 0, False)
        rate = matrix_rate * math.sqrt(max(weight.shape[0] * dp_count, weight.shape[1]))
        new_weights.append(weight - rate * update[:, : weight.shape[1]].astype(f32))
    mean_next = beta_first * gain_mean + (1.0 - beta_first) * gain_grad
    var_next = beta_second * gain_var + (1.0 - beta_second) * gain_grad * gain_grad
    gains_next = norm_gains - gain_rate * (mean_next / first_fix) / (
        jnp.sqrt(var_next / second_fix) + adam_eps
    )
    return (
        output.astype(bf16)[None],
        grad_input[None],
        *grads,
        gain_grad,
        *new_weights,
        gains_next,
        *moments_next,
        mean_next,
        var_next,
    )


def fits_pairs(mesh):
    dp_count, ctx_count = mesh.shape["dp"], mesh.shape["ctx"]
    return ctx_count == 2 and HEADS % 4 == 0 and dp_count % 8 == 0


def solution(mesh):
    placed = (
        P("dp", "ctx", None),
        P("dp", "ctx", None),
        P("dp", "ctx"),
        P("dp", None),
        P("dp", None),
        P("dp", None),
        P("dp", None),
        P(None, "dp"),
        P("dp", None),
        P("dp", None),
        P("dp", None),
        P("dp", None),
        P(None, "dp"),
        P(None, "dp"),
    )
    body = per_device
    if fits_pairs(mesh):
        body = functools.partial(paired_device, ring_places(mesh))
    return jax.shard_map(
        body,
        mesh=mesh,
        in_specs=placed,
        out_specs=(
            P("dp", "ctx", None),
            P("dp", "ctx", None),
            P("dp", None),
            P("dp", None),
            P("dp", None),
            P("dp", None),
            P(None, "dp"),
            P("dp", None),
            P("dp", None),
            P("dp", None),
            P("dp", None),
            P(None, "dp"),
            P("dp", None),
            P("dp", None),
            P("dp", None),
            P("dp", None),
            P(None, "dp"),
            P(None, "dp"),
        ),
        check_vma=False,
    )
```
